32 devices in a mesh: groups: 2 (over y), seq: 4 (over z), mp: 2 (over x), sub: 2 (over core).
Axes of the slice: x: 2, y: 2, z: 4, core: 2. Of those that a mesh axis runs over, the one named last changes fastest.
Arguments:
- seq_in: bfloat16 [4096, 1536], P(('groups', 'seq'), ('mp', 'sub')), parts along dimension 0, may hold values from -48 to 48
- conv_gain: float32 [3, 1536], replicated, may hold values from 0.1 to 1.9
- conv_weight: bfloat16 [3, 3, 1536, 1536], P(None, None, None, ('mp', 'sub')), may hold values from -0.09375 to 0.09375
- w_q: bfloat16 [1536, 1024], P(None, 'mp'), may hold values from -0.102062073 to 0.102062073
- w_k: bfloat16 [1536, 1024], P(None, 'mp'), may hold values from -0.102062073 to 0.102062073
- w_v: bfloat16 [1536, 1024], P(None, 'mp'), may hold values from -0.15625 to 0.15625
- w_o: bfloat16 [1024, 1536], P('mp'), may hold values from -0.1875 to 0.1875
Outputs:
- seq_out: bfloat16 [4096, 1536], P(('groups', 'seq', 'sub'), 'mp'), parts along dimension 0
The draws below stay inside these ranges and needn't reach their ends.
There are 2 independent parts, one for each index of `groups`. The reference program is written for one: setup_inputs(seed, part) draws one part's arguments, and reference() takes and returns one part's arrays. A program takes and returns all parts, laid end to end along the dimension named above; an argument that names none is the same for every part. Nothing has to cross between parts.
All inputs are finite; a program needn't handle non-finite values.
Results may differ from the reference program's by a relative error of at most 0.015.
Values may be sent and summed in bfloat16 or wider, within the bound.
No kernel may reach another device: no remote copies, remote signals or barrier semaphores. Data moves between devices by JAX's collectives and lax.ppermute only.
A program may use at most 128 MiB of HBM per device.

```python
import math
import jax
import jax.numpy as jnp
from jax import lax

C = 1536
HEADS = 8
HEAD = 128
LAYERS = 3
BINS_DEV = 512
SEQ_LEN = 2048


def draw_seq_in(key, part):
    base = jnp.clip(jax.random.normal(key, (SEQ_LEN, C), jnp.float32), -8.0, 8.0)
    return base.astype(jnp.bfloat16)


def key_matrix(key):
    drawn = jax.random.normal(jax.random.fold_in(key, 11), (C, HEADS * HEAD), jnp.float32)
    return jnp.clip(drawn, -4.0, 4.0) / math.sqrt(C)


def draw_w_k(key, part):
    return key_matrix(key).astype(jnp.bfloat16)


def draw_w_q(key, part):
    drawn = jax.random.normal(jax.random.fold_in(key, 23), (C, HEADS * HEAD), jnp.float32)
    fresh = jnp.clip(drawn, -4.0, 4.0) / math.sqrt(C)
    return fresh.astype(jnp.bfloat16)


def steps_of(own_key, dims, pieces, smallest, largest):
    def one(position, blocks):
        heights = jax.random.uniform(jax.random.fold_in(jax.random.fold_in(own_key, 6), position), (blocks,), jnp.float32, smallest / len(pieces), largest / len(pieces))
        return jnp.repeat(jnp.exp(heights), dims[position] // blocks).reshape((-1,) + (1,) * (len(dims) - position - 1))

    factor_of = one(*pieces[0])
    for cut in pieces[1:]:
        factor_of = factor_of * one(*cut)
    return factor_of


def normal_values(stream_key, shape, spread, most, pieces=(), held_as=jnp.bfloat16):
    result = spread * jax.random.normal(stream_key, shape, jnp.float32)
    if pieces:
        result = result * steps_of(stream_key, shape, pieces, -0.22, 0.18)
    return jnp.clip(result, -most, most).astype(held_as)


def setup_inputs(seed: int = 0, part: int = 0) -> dict:
    key_of = jax.random.split(jax.random.key(seed), 8)
    part_splits = jax.random.split(jax.random.fold_in(key_of[7], part), 8)
    return {
        "seq_in": draw_seq_in(jax.random.fold_in(jax.random.fold_in(key_of[7], part), 71), part),
        "conv_gain": jnp.clip(1.0 + 0.18 * jax.random.normal(key_of[1], (LAYERS, C), jnp.float32), 0.1, 1.9),
        "conv_weight": normal_values(key_of[2], (LAYERS, 3, C, C), (3 * C) ** -0.5, 0.09375, ((3, 4),)),
        "w_q": draw_w_q(jax.random.fold_in(key_of[7], 71), part),
        "w_k": draw_w_k(jax.random.fold_in(key_of[7], 71), part),
        "w_v": normal_values(key_of[5], (C, HEADS * HEAD), C ** -0.5, 0.15625, ((1, 2),)),
        "w_o": normal_values(key_of[6], (HEADS * HEAD, C), (HEADS * HEAD) ** -0.5, 0.1875, ((0, 2),)),
    }


def reference(seq_in, conv_gain, conv_weight, w_q, w_k, w_v, w_o):
    dilations = (BINS_DEV // 4, BINS_DEV, 2 * BINS_DEV)
    stream = seq_in
    for section_index in range(LAYERS):
        widened = stream.astype(jnp.float32)
        normed = widened * lax.rsqrt(lax.optimization_barrier(jnp.mean(widened * widened, axis=1, keepdims=True)) + 1e-06) * conv_gain[section_index]
        hidden = jax.nn.gelu(normed).astype(jnp.bfloat16)
        dilation = dilations[section_index]
        first_tap = jnp.dot(hidden, conv_weight[section_index, 0], preferred_element_type=jnp.float32)
        middle_tap = jnp.dot(hidden, conv_weight[section_index, 1], preferred_element_type=jnp.float32)
        last_tap = jnp.dot(hidden, conv_weight[section_index, 2], preferred_element_type=jnp.float32)
        padding = jnp.zeros((dilation, C), jnp.float32)
        before = jnp.concatenate([padding, first_tap[:SEQ_LEN - dilation]], axis=0)
        after = jnp.concatenate([last_tap[dilation:], padding], axis=0)
        stream = (widened + before + middle_tap + after).astype(jnp.bfloat16)
    queries = jnp.dot(stream, w_q, preferred_element_type=jnp.float32).astype(jnp.bfloat16).reshape(SEQ_LEN, HEADS, HEAD)
    keys = jnp.dot(stream, w_k, preferred_element_type=jnp.float32).astype(jnp.bfloat16).reshape(SEQ_LEN, HEADS, HEAD)
    values = jnp.dot(stream, w_v, preferred_element_type=jnp.float32).astype(jnp.bfloat16).reshape(SEQ_LEN, HEADS, HEAD)
    score_scale = 1.0 / math.sqrt(HEAD)
    block_rows = math.gcd(SEQ_LEN, 512)
    keys_wide = keys.astype(jnp.float32)
    values_wide = values.astype(jnp.float32)

    def attend_block(query_block):
        scores = jnp.einsum('qhe,khe->hqk', query_block.astype(jnp.float32), keys_wide) * score_scale
        top_score = lax.optimization_barrier(jnp.max(scores, axis=-1, keepdims=True))
        expw = jnp.exp(scores - top_score)
        denom = lax.optimization_barrier(jnp.sum(expw, axis=-1))
        weights = lax.optimization_barrier(expw.astype(jnp.bfloat16)).astype(jnp.float32)
        numer = jnp.einsum('hqk,khe->qhe', weights, values_wide)
        return (numer / denom.T[:, :, None]).astype(jnp.bfloat16)
    blocks = queries.reshape(SEQ_LEN // block_rows, block_rows, HEADS, HEAD)
    attended = lax.map(attend_block, blocks).reshape(SEQ_LEN, HEADS * HEAD)
    mixed = jnp.dot(attended, w_o, preferred_element_type=jnp.float32)
    return (stream.astype(jnp.float32) + mixed).astype(jnp.bfloat16)
```

```python
import functools
import math

import jax
import jax.numpy as jnp
from jax import lax
from jax.experimental import pallas as pl
from jax.experimental.pallas import tpu as pltpu
from jax.sharding import PartitionSpec as P

HEAD = 128
LAYERS = 3
BINS_DEV = 512
F32 = jnp.float32
BF16 = jnp.bfloat16
VMEM_LIMIT = 48 * 1024 * 1024


def swap(x, axis):
    return lax.ppermute(x, axis, [(0, 1), (1, 0)])


def swap_both(x):
    return lax.ppermute(x, ("mp", "sub"), [(i, 3 - i) for i in range(4)])


def rotate(x, by):
    n = lax.axis_size("seq")
    return lax.ppermute(x, "seq", [(i, (i + by) % n) for i in range(n)])


def gather_parts(x):
    across = swap(x, "mp")
    return x, swap(x, "sub"), across, swap(across, "sub")


def fill_hidden(scalars, parts, gain_ref, hidden):
    width = parts[0].shape[-1]
    wide = [part[...].astype(F32) for part in parts]
    squares = wide[0] * wide[0]
    for x in wide[1:]:
        squares = squares + x * x
    mean = jnp.sum(squares, axis=1, keepdims=True) / (4 * width)
    scale = lax.rsqrt(mean + 1e-06)
    for p, x in enumerate(wide):
        columns = pl.ds(pl.multiple_of(scalars[p] * width, 128), width)
        normed = x * scale * gain_ref[0, :, columns]
        hidden[:, columns] = jax.nn.gelu(normed).astype(BF16)


def dot(a, b):
    return jnp.dot(a, b, preferred_element_type=F32)


def first_edge_kernel(scalars, p0, p1, p2, p3, gain, w, acc, up, down, hidden):
    tap = pl.program_id(0)
    b = up.shape[0]

    @pl.when(tap == 0)
    def _():
        fill_hidden(scalars, (p0, p1, p2, p3), gain, hidden)

    terms = dot(hidden[...], w[0, 0])

    @pl.when(tap == 0)
    def _():
        acc[1] = terms[:b]
        up[...] = terms[b:].astype(BF16)

    @pl.when(tap == 1)
    def _():
        acc[0] = terms[:b]
        acc[3] = terms[b:]

    @pl.when(tap == 2)
    def _():
        down[...] = terms[:b].astype(BF16)
        acc[2] = terms[b:]


def first_middle_kernel(
    scalars, p0, p1, p2, p3, edge, gain, w, acc_in, lower, upper, out, hidden, acc
):
    tap = pl.program_id(0)
    b = lower.shape[0]

    @pl.when(tap == 0)
    def _():
        fill_hidden(scalars, (p0, p1, p2, p3), gain, hidden)

    terms = dot(hidden[...], w[0, 0])

    @pl.when(tap == 0)
    def _():
        acc[0] = acc_in[2] + terms[:b]
        out[3] = (
            edge[b:].astype(F32) + acc_in[3] + upper[...].astype(F32) + terms[b:]
        ).astype(BF16)

    @pl.when(tap == 1)
    def _():
        acc[1] = acc_in[1] + terms[:b]
        acc[0] = acc[0] + terms[b:]

    @pl.when(tap == 2)
    def _():
        out[0] = (
            edge[:b].astype(F32) + acc_in[0] + lower[...].astype(F32) + terms[:b]
        ).astype(BF16)
        out[1] = (p0[:b].astype(F32) + acc[1] + terms[b:]).astype(BF16)
        out[2] = (p0[b:].astype(F32) + acc[0]).astype(BF16)


def second_early_kernel(scalars, p0, p1, p2, p3, gain, w, acc, hidden):
    tap = pl.program_id(0)
    b = p0.shape[0] // 2

    @pl.when(tap == 0)
    def _():
        acc[...] = jnp.zeros_like(acc)
        fill_hidden(scalars, (p0, p1, p2, p3), gain, hidden)

    terms = dot(hidden[...], w[0, 0])
    for i in range(2):
        place = scalars[4 + i] + 2 - tap
        acc[place] = acc[place] + terms[i * b : (i + 1) * b]


def second_late_kernel(
    scalars, p0, p1, p2, p3, early, gain, w, acc_in, even, odd, hidden, acc, kept
):
    tap = pl.program_id(0)
    b = p0.shape[0] // 2

    @pl.when(tap == 0)
    def _():
        acc[...] = acc_in[...]
        for i in range(2):
            kept[scalars[4 + i]] = early[i * b : (i + 1) * b]
            kept[scalars[6 + i]] = p0[i * b : (i + 1) * b]
        fill_hidden(scalars, (p0, p1, p2, p3), gain, hidden)

    terms = dot(hidden[...], w[0, 0])
    for i in range(2):
        place = scalars[6 + i] + 2 - tap
        acc[place] = acc[place] + terms[i * b : (i + 1) * b]

    @pl.when(tap == 2)
    def _():
        for k in range(4):
            out = even if k % 2 == 0 else odd
            half = pl.ds((k // 2) * b, b)
            out[half, :] = (kept[k].astype(F32) + acc[k + 1]).astype(BF16)


def third_kernel(scalars, p0, p1, p2, p3, gain, w, out, hidden, acc):
    step = pl.program_id(0)
    b = p0.shape[0] // 2

    @pl.when(step == 0)
    def _():
        fill_hidden(scalars, (p0, p1, p2, p3), gain, hidden)
        acc[...] = p0[...].astype(F32) + dot(hidden[...], w[0, 0])

    @pl.when(step == 1)
    def _():
        acc[:b] = acc[:b] + dot(hidden[b:], w[0, 0])

    @pl.when(step == 2)
    def _():
        acc[b:] = acc[b:] + dot(hidden[:b], w[0, 0])
        out[...] = acc[...].astype(BF16)


def project_kernel(scalars, p0, p1, p2, p3, w_q, w_k, w_v, out, rows):
    width = p0.shape[1]
    for p, part in enumerate((p0, p1, p2, p3)):
        rows[:, pl.ds(pl.multiple_of(scalars[p] * width, 128), width)] = part[...]
    for i, w in enumerate((w_q, w_k, w_v)):
        made = dot(rows[...], w[...]).astype(BF16)
        for h in range(out.shape[0]):
            out[h, :, i * HEAD : (i + 1) * HEAD] = made[:, h * HEAD : (h + 1) * HEAD]


def attend_kernel(scalars, *refs):
    own, other = refs[:8], refs[8:16]
    out, queries, keys, values = refs[16:]
    b = own[0].shape[0]
    sub = scalars[8]
    z = scalars[9]
    for c in range(2):
        for s in range(4):
            i = c * 4 + s
            queries[c, sub, s] = own[i][:, :HEAD]
            queries[c, 1 - sub, s] = other[i][:, :HEAD]
            for o, ref in enumerate((own[i], other[i])):
                here = pl.ds((i * 2 + o) * b, b)
                keys[here, :] = ref[:, HEAD : 2 * HEAD]
                values[here, :] = ref[:, 2 * HEAD :]
    factor = math.log2(math.e) / math.sqrt(HEAD)
    for k in range(4):
        for a in range(2):
            s = lax.rem(z - 2 * sub - a + 4, 4)
            q = queries[k % 2, k // 2, s]
            scores = lax.dot_general(
                q, keys[...], (((1,), (1,)), ((), ())), preferred_element_type=F32
            )
            top = jnp.max(scores, axis=1, keepdims=True)
            expw = jnp.exp2((scores - top) * factor)
            denom = jnp.sum(expw, axis=1, keepdims=True)
            numer = dot(expw.astype(BF16), values[...])
            out[k, a * b : (a + 1) * b, :] = (numer / denom).astype(BF16)


def finish_kernel(scalars, *refs):
    own, other, rest = refs[:4], refs[4:8], refs[8:12]
    w_own, w_near, w_far, out, mixed, residual = refs[12:]
    sub, z = scalars[8], scalars[9]
    b, width = rest[0].shape
    half = 4 * HEAD
    for s in range(4):
        head = lax.rem(z - s + 4, 4)
        mixed[:, pl.ds(pl.multiple_of(head * HEAD, HEAD), HEAD)] = own[s][...]
        place = lax.rem(head + 2 * (1 - sub) + 2, 4)
        mixed[:, pl.ds(pl.multiple_of(half + place * HEAD, HEAD), HEAD)] = other[s][...]
        turn = lax.rem(z - s + 4, 4)
        rows = pl.ds(pl.multiple_of((turn // 2) * b, b), b)
        columns = pl.ds(pl.multiple_of(lax.rem(turn, 2) * width, 128), width)
        residual[rows, columns] = rest[s][...]
    shares = dot(mixed[:, :half], w_own[...])
    shares = shares + dot(mixed[:, half : half + 2 * HEAD], w_near[...])
    shares = shares + dot(mixed[:, half + 2 * HEAD :], w_far[...])
    out[...] = (residual[...].astype(F32) + shares).astype(BF16)


def whole(x):
    zeros = (0,) * x.ndim
    return pl.BlockSpec(x.shape, lambda *_: zeros)


def call(kernel, scalars, args, outs, scratch, grid=(1,), specs=None, flops=0):
    specs = specs or {}
    in_specs = [specs.get(i, None) or whole(a) for i, a in enumerate(args)]
    moved = sum(a.size * a.dtype.itemsize for i, a in enumerate(args) if i not in specs)
    moved += sum(math.prod(o.shape) * o.dtype.itemsize for o in outs)
    single = len(outs) == 1
    return pl.pallas_call(
        kernel,
        out_shape=outs[0] if single else outs,
        grid_spec=pltpu.PrefetchScalarGridSpec(
            num_scalar_prefetch=1,
            grid=grid,
            in_specs=in_specs,
            out_specs=whole(outs[0]) if single else [whole(o) for o in outs],
            scratch_shapes=scratch,
        ),
        compiler_params=pltpu.CompilerParams(
            dimension_semantics=("arbitrary",) * len(grid), vmem_limit_bytes=VMEM_LIMIT
        ),
        cost_estimate=pl.CostEstimate(flops=flops, transcendentals=0, bytes_accessed=moved),
        name=kernel.__name__,
    )(scalars, *args)


def struct(shape, dtype=BF16):
    return jax.ShapeDtypeStruct(shape, dtype)


def pick(x, index):
    return lax.dynamic_index_in_dim(x, index, 0, keepdims=False)


def per_device_fast(seq_in, conv_gain, conv_weight, w_q, w_k, w_v, w_o):
    rows, width = seq_in.shape
    channels = 4 * width
    n = 4
    b = rows // n
    z, mp, sub = (lax.axis_index(a) for a in ("seq", "mp", "sub"))
    place = mp * 2 + sub
    turns = [lax.rem(z - s + n, n) for s in range(n)]
    scalars = jnp.stack(
        [place, place ^ 1, place ^ 2, place ^ 3] + turns + [sub, z, mp]
    ).astype(jnp.int32)
    gains = conv_gain.reshape(LAYERS, 1, channels)
    hidden = pltpu.VMEM((2 * b, channels), BF16)

    def tap_specs(layer, at_gain, at_w, first=0):
        return {
            at_gain: pl.BlockSpec((1, 1, channels), lambda j, _: (layer, 0, 0)),
            at_w: pl.BlockSpec(
                (1, 1, channels, width), lambda j, _: (layer, lax.rem(j + first, 3), 0, 0)
            ),
        }

    flops = 2 * 2 * b * channels * 3 * width

    edge = jnp.concatenate([seq_in[:b], seq_in[3 * b :]], axis=0)
    middle = seq_in[b : 3 * b]
    edge_parts = gather_parts(edge)
    middle_parts = gather_parts(middle)
    acc, up, down = call(
        first_edge_kernel,
        scalars,
        (*edge_parts, gains, conv_weight),
        [struct((n, b, width), F32), struct((b, width)), struct((b, width))],
        [hidden],
        grid=(3,),
        specs=tap_specs(0, 4, 5),
        flops=flops,
    )
    lower = lax.ppermute(up, "seq", [(i, i + 1) for i in range(n - 1)])
    upper = lax.ppermute(down, "seq", [(i + 1, i) for i in range(n - 1)])
    stream = call(
        first_middle_kernel,
        scalars,
        (*middle_parts, edge, gains, conv_weight, acc, lower, upper),
        [struct((n, b, width))],
        [hidden, pltpu.VMEM((2, b, width), F32)],
        grid=(3,),
        specs=tap_specs(0, 5, 6),
        flops=flops,
    )

    dealt = [pick(stream, z)]
    for s in range(1, n):
        dealt.append(rotate(pick(stream, lax.rem(z + s, n)), s))

    early = jnp.concatenate(dealt[:2], axis=0)
    late = jnp.concatenate(dealt[2:], axis=0)
    early_parts = gather_parts(early)
    late_parts = gather_parts(late)
    acc = call(
        second_early_kernel,
        scalars,
        (*early_parts, gains, conv_weight),
        [struct((n + 2, b, width), F32)],
        [hidden],
        grid=(3,),
        specs=tap_specs(1, 4, 5),
        flops=flops,
    )
    pairs = call(
        second_late_kernel,
        scalars,
        (*late_parts, early, gains, conv_weight, acc),
        [struct((2 * b, width)), struct((2 * b, width))],
        [hidden, pltpu.VMEM((n + 2, b, width), F32), pltpu.VMEM((n, b, width), BF16)],
        grid=(3,),
        specs=tap_specs(1, 5, 6),
        flops=flops,
    )

    out_width = w_o.shape[1] // 2
    half_rows = w_o.shape[0] // 2
    asked = lax.dynamic_slice(
        w_o, (sub * half_rows, (1 - mp) * out_width), (half_rows, out_width)
    )
    w_near = swap(asked, "mp")
    w_far = swap(w_near, "sub")

    final = [
        call(
            third_kernel,
            scalars,
            (*gather_parts(pair), gains, conv_weight),
            [struct((2 * b, width))],
            [hidden, pltpu.VMEM((2 * b, width), F32)],
            grid=(3,),
            specs=tap_specs(2, 4, 5, first=1),
            flops=flops * 2 // 3,
        )
        for pair in pairs
    ]

    received = []
    for pair in final:
        halves = pair.reshape(2, b, width)
        mine, theirs = pick(halves, sub), pick(halves, 1 - sub)
        projected = call(
            project_kernel,
            scalars,
            (mine, swap(theirs, "sub"), swap(mine, "mp"), swap_both(theirs), w_q, w_k, w_v),
            [struct((n, b, 3 * HEAD))],
            [pltpu.VMEM((b, channels), BF16)],
            flops=2 * b * channels * 3 * n * HEAD,
        )
        received.append(pick(projected, z))
        for s in range(1, n):
            received.append(rotate(pick(projected, lax.rem(z + s, n)), s))
    swapped = [swap(x, "sub") for x in received]
    attended = call(
        attend_kernel,
        scalars,
        (*received, *swapped),
        [struct((n, 2 * b, HEAD))],
        [
            pltpu.VMEM((2, 2, n, b, HEAD), BF16),
            pltpu.VMEM((16 * b, HEAD), BF16),
            pltpu.VMEM((16 * b, HEAD), BF16),
        ],
        flops=4 * 8 * b * 16 * b * HEAD,
    )

    kept = [final[0][:b], final[1][:b], final[0][b:], final[1][b:]]
    kept = jnp.stack(kept)
    rest = []
    for s in range(n):
        steps = [(2 * (i % 2) + j + s) % n for i in range(n) for j in range(2)]
        pairs_of = [(i * 2 + j, steps[i * 2 + j] * 2 + i // 2) for i in range(n) for j in range(2)]
        target = lax.rem(2 * lax.rem(z, 2) + sub + s, n)
        rest.append(lax.ppermute(pick(kept, target), ("seq", "sub"), pairs_of))

    heads = [pick(attended, z)]
    for s in range(1, n):
        heads.append(rotate(pick(attended, lax.rem(z + s, n)), s))
    others = [swap(x, "mp") for x in heads]
    args = (*heads, *others, *rest, w_o, w_near, w_far)
    return call(
        finish_kernel,
        scalars,
        args,
        [struct((2 * b, out_width))],
        [pltpu.VMEM((2 * b, 8 * HEAD), BF16), pltpu.VMEM((2 * b, out_width), BF16)],
        specs={12: pl.BlockSpec((n * HEAD, out_width), lambda i, ids: (0, ids[10]))},
        flops=2 * 2 * b * 8 * HEAD * out_width,
    )


def passed_along(x, axis, by):
    devices = lax.axis_size(axis)
    pairs = [(i, i + by) for i in range(devices) if 0 <= i + by < devices]
    return lax.ppermute(x, axis, pairs)


def tower_section(stream_shard, gain_row, weight_taps, dilation):
    rows_here = stream_shard.shape[0]
    gathered = lax.all_gather(stream_shard, ("mp", "sub"), axis=1, tiled=True)
    widened = gathered.astype(jnp.float32)
    normed = (
        widened * lax.rsqrt(jnp.mean(widened * widened, axis=1, keepdims=True) + 1e-06) * gain_row
    )
    hidden = jax.nn.gelu(normed).astype(jnp.bfloat16)
    tap_terms = jnp.einsum("rc,jco->jro", hidden, weight_taps, preferred_element_type=jnp.float32)
    span_rows = min(dilation, rows_here)
    hop_count = max(dilation // rows_here, 1)
    lower_part = passed_along(
        tap_terms[0, rows_here - span_rows :].astype(jnp.bfloat16), "seq", hop_count
    ).astype(jnp.float32)
    upper_part = passed_along(
        tap_terms[2, :span_rows].astype(jnp.bfloat16), "seq", -hop_count
    ).astype(jnp.float32)
    before = jnp.concatenate([lower_part, tap_terms[0, : rows_here - span_rows]], axis=0)
    after = jnp.concatenate([tap_terms[2, span_rows:], upper_part], axis=0)
    return (stream_shard.astype(jnp.float32) + before + tap_terms[1] + after).astype(jnp.bfloat16)


def per_device(seq_in, conv_gain, conv_weight, w_q, w_k, w_v, w_o):
    rows_here = seq_in.shape[0]
    dilations = (BINS_DEV // 4, BINS_DEV, 2 * BINS_DEV)
    stream = seq_in
    for section_index in range(LAYERS):
        stream = tower_section(
            stream, conv_gain[section_index], conv_weight[section_index], dilations[section_index]
        )
    query_rows = rows_here // lax.axis_size("sub")
    mp_width = w_o.shape[1] // lax.axis_size("mp")
    widest = lax.all_gather(stream, ("mp", "sub"), axis=1, tiled=True)
    query_inputs = lax.dynamic_slice_in_dim(
        widest, lax.axis_index("sub") * query_rows, query_rows, 0
    )
    residual_part = lax.dynamic_slice_in_dim(
        query_inputs, lax.axis_index("mp") * mp_width, mp_width, 1
    )
    heads_here = w_q.shape[1] // HEAD
    queries = (
        jnp.dot(query_inputs, w_q, preferred_element_type=jnp.float32)
        .astype(jnp.bfloat16)
        .reshape(query_rows, heads_here, HEAD)
    )
    keys = (
        jnp.dot(query_inputs, w_k, preferred_element_type=jnp.float32)
        .astype(jnp.bfloat16)
        .reshape(query_rows, heads_here, HEAD)
    )
    values = (
        jnp.dot(query_inputs, w_v, preferred_element_type=jnp.float32)
        .astype(jnp.bfloat16)
        .reshape(query_rows, heads_here, HEAD)
    )
    score_scale = 1.0 / math.sqrt(HEAD)
    running_top = jnp.full((heads_here, query_rows), -1e30, jnp.float32)
    running_numer = jnp.zeros((query_rows, heads_here, HEAD), jnp.float32)
    key_rows = lax.all_gather(keys, ("seq", "sub"), axis=0, tiled=True)
    value_rows = lax.all_gather(values, ("seq", "sub"), axis=0, tiled=True)
    scores = (
        jnp.einsum("qhe,khe->hqk", queries, key_rows, preferred_element_type=jnp.float32)
        * score_scale
    )
    new_top = jnp.maximum(running_top, jnp.max(scores, axis=-1))
    expw = jnp.exp(scores - new_top[:, :, None])
    factor = jnp.exp(running_top - new_top)
    new_denom = jnp.sum(expw, axis=-1)
    contrib = jnp.einsum(
        "hqk,khe->qhe", expw.astype(jnp.bfloat16), value_rows, preferred_element_type=jnp.float32
    )
    new_numer = running_numer * factor.T[:, :, None] + contrib
    attended = (
        (new_numer / new_denom.T[:, :, None])
        .astype(jnp.bfloat16)
        .reshape(query_rows, heads_here * HEAD)
    )
    column_weight = lax.all_to_all(w_o, "mp", split_axis=1, concat_axis=0, tiled=True)
    every_head = lax.all_gather(attended, "mp", axis=1, tiled=True)
    shares = jnp.dot(every_head, column_weight, preferred_element_type=jnp.float32)
    return (residual_part.astype(jnp.float32) + shares).astype(jnp.bfloat16)


def solution(mesh):
    placed = (
        P(("groups", "seq"), ("mp", "sub")),
        P(),
        P(None, None, None, ("mp", "sub")),
        P(None, "mp"),
        P(None, "mp"),
        P(None, "mp"),
        P("mp", None),
    )
    sizes = dict(mesh.shape)
    dealt = sizes["seq"] == 4 and sizes["mp"] == 2 and sizes["sub"] == 2
    return jax.shard_map(
        per_device_fast if dealt else per_device,
        mesh=mesh,
        in_specs=placed,
        out_specs=P(("groups", "seq", "sub"), "mp"),
        check_vma=False,
    )
```

```python
import functools
import math

import jax
import jax.numpy as jnp
from jax import lax
from jax.experimental import pallas as pl
from jax.experimental.pallas import tpu as pltpu
from jax.sharding import PartitionSpec as P

HEAD = 128
LAYERS = 3
BINS_DEV = 512
F32 = jnp.float32
BF16 = jnp.bfloat16
VMEM_LIMIT = 16 * 1024 * 1024
SPLIT = 4


def swap(x, axis):
    return lax.ppermute(x, axis, [(0, 1), (1, 0)])


def swap_both(x):
    return lax.ppermute(x, ("mp", "sub"), [(i, 3 - i) for i in range(4)])


def rotate(x, by):
    n = lax.axis_size("seq")
    return lax.ppermute(x, "seq", [(i, (i + by) % n) for i in range(n)])


def gather_parts(*pieces, under=None):
    across = [swap(x, "mp") for x in pieces]
    if under is not None:
        across = lax.optimization_barrier((across, under))[0]
    near = [swap(x, "sub") for x in pieces]
    return (*pieces, *near, *across, *[swap(x, "sub") for x in across])


def dot(a, b):
    return jnp.dot(a, b, preferred_element_type=F32)


def at(start, size):
    return pl.ds(pl.multiple_of(start, size), size)


SUB, SEQ = 4, 5


def fill_hidden(scalars, parts, gains, layer, hidden, order=None):
    count = len(parts) // 4
    rows, width = parts[0].shape
    quarter = rows * count // 4
    tile = 16
    columns = [at(scalars[p] * width, width) for p in range(4)]
    gain = [gains[layer : layer + 1, c] for c in columns]
    for r in range(0, rows * count, tile):
        here = slice(r % rows, r % rows + tile)
        wide = [parts[p * count + r // rows][here, :].astype(F32) for p in range(4)]
        squares = wide[0] * wide[0]
        for x in wide[1:]:
            squares = squares + x * x
        mean = jnp.sum(squares, axis=1, keepdims=True) / (4 * width)
        scale = lax.rsqrt(mean + 1e-06)
        if order is None:
            target = pl.ds(r, tile)
        else:
            target = at(order[r // quarter] * quarter + r % quarter, tile)
        for p, x in enumerate(wide):
            hidden[target, columns[p]] = jax.nn.gelu(x * scale * gain[p]).astype(BF16)


def turn(scalars, by):
    return lax.rem(scalars[SEQ] + by, 4)


def bring(copies):
    copies = [pltpu.make_async_copy(*copy) for copy in copies]
    for copy in copies:
        copy.start()
    for copy in copies:
        copy.wait()


def load_taps_kernel(layer, scalars, w, out, sems):
    size = out.shape[1] // SPLIT
    copies = []
    for tap in range(3):
        for i in range(SPLIT):
            rows = pl.ds(i * size, size)
            copies.append((w.at[layer, tap, rows], out.at[tap, rows], sems.at[tap, i]))
    bring(copies)


def load_projections_kernel(scalars, w_q, w_k, w_v, out, sems):
    size = out.shape[1] // SPLIT
    copies = []
    for m, w in enumerate((w_q, w_k, w_v)):
        for i in range(SPLIT):
            rows = pl.ds(i * size, size)
            copies.append((w.at[rows], out.at[m, rows], sems.at[m, i]))
    bring(copies)


def cut_kernel(scalars, x, edge, middle, sems):
    b = edge.shape[0] // 2
    bring(
        [
            (x.at[pl.ds(0, b)], edge.at[pl.ds(0, b)], sems.at[0]),
            (x.at[pl.ds(3 * b, b)], edge.at[pl.ds(b, b)], sems.at[1]),
            (x.at[pl.ds(b, 2 * b)], middle, sems.at[2]),
        ]
    )


def first_edge_kernel(scalars, p0, p1, p2, p3, gains, w, acc, up, down, hidden):
    fill_hidden(scalars, (p0, p1, p2, p3), gains, 0, hidden)
    b = up.shape[0]
    middle = p0[...].astype(F32) + dot(hidden[...], w[1])
    before = dot(hidden[...], w[0])
    after = dot(hidden[...], w[2])
    up[...] = before[b:].astype(BF16)
    down[...] = after[:b].astype(BF16)
    acc[0] = middle[:b]
    acc[1] = before[:b]
    acc[2] = after[b:]
    acc[3] = middle[b:]


def first_middle_kernel(
    scalars, p0, p1, p2, p3, gains, w, acc, partial, hidden
):
    fill_hidden(scalars, (p0, p1, p2, p3), gains, 0, hidden)
    b = acc.shape[1]
    middle = p0[...].astype(F32) + dot(hidden[...], w[1])
    before = dot(hidden[...], w[0])
    after = dot(hidden[...], w[2])
    partial[0] = acc[0] + after[:b]
    partial[1] = acc[1] + middle[:b] + after[b:]
    partial[2] = acc[2] + middle[b:] + before[:b]
    partial[3] = acc[3] + before[b:]


def deal_kernel(scalars, partial, lower, upper, *refs):
    outs, stream = refs[:4], refs[4]
    stream[0] = (partial[0] + lower[...].astype(F32)).astype(BF16)
    stream[1] = partial[1].astype(BF16)
    stream[2] = partial[2].astype(BF16)
    stream[3] = (partial[3] + upper[...].astype(F32)).astype(BF16)
    for s, out in enumerate(outs):
        out[...] = stream[turn(scalars, s)]


def local_taps(hidden, acc, w, shift):
    rows = hidden.shape[0]
    acc[...] = dot(hidden[...], w[1])
    acc[shift:, :] += dot(hidden[: rows - shift, :], w[0])
    acc[: rows - shift, :] += dot(hidden[shift:, :], w[2])


def second_kernel(scalars, *refs):
    parts = refs[:8]
    gains, w, low, high, hidden, acc, kept = refs[8:]
    half = low.shape[0]
    b = half // 2
    order = [turn(scalars, 4 - s) for s in range(4)]
    fill_hidden(scalars, parts, gains, 1, hidden, order)
    for s in range(4):
        kept[order[s]] = parts[s // 2][(s % 2) * b : (s % 2 + 1) * b, :]
    local_taps(hidden, acc, w, b)
    for k in range(4):
        out = low if k < 2 else high
        made = kept[k].astype(F32) + acc[k * b : (k + 1) * b, :]
        out[(k % 2) * b : (k % 2 + 1) * b, :] = made.astype(BF16)


def third_kernel(scalars, *refs):
    parts = refs[:8]
    gains, w = refs[8:10]
    mine, theirs = refs[10:12]
    outs = refs[12:16]
    hidden, acc, made = refs[16:]
    half = parts[0].shape[0]
    b = half // 2
    fill_hidden(scalars, parts, gains, 2, hidden)
    local_taps(hidden, acc, w, half)
    for k in range(4):
        own = parts[k // 2][(k % 2) * b : (k % 2 + 1) * b, :].astype(F32)
        made[k] = (own + acc[k * b : (k + 1) * b, :]).astype(BF16)
    sub = scalars[SUB]
    for c in range(2):
        rows = slice(c * b, (c + 1) * b)
        mine[rows, :] = made[2 * c + sub]
        theirs[rows, :] = made[2 * c + 1 - sub]
    for s, out in enumerate(outs):
        out[...] = made[turn(scalars, s)]


def sort_kernel(scalars, *refs):
    arrived, keep, give, ordered = refs[:4], *refs[4:]
    b = arrived[0].shape[0]
    for s in range(4):
        ordered[turn(scalars, 4 - s)] = arrived[s][...]
    for a in range(2):
        rows = slice(a * b, (a + 1) * b)
        keep[rows, :] = ordered[2 * scalars[SUB] + a]
        give[rows, :] = ordered[2 * (1 - scalars[SUB]) + a]


def project_kernel(scalars, p0, p1, p2, p3, w, o0, o1, o2, o3, rows, made):
    width = p0.shape[1]
    for p, part in enumerate((p0, p1, p2, p3)):
        rows[:, at(scalars[p] * width, width)] = part[...]
    for i in range(3):
        product = dot(rows[...], w[i]).astype(BF16)
        for h in range(4):
            made[h, :, i * HEAD : (i + 1) * HEAD] = product[:, h * HEAD : (h + 1) * HEAD]
    for s, out in enumerate((o0, o1, o2, o3)):
        out[...] = made[turn(scalars, s)]


def attend_kernel(scalars, *refs):
    own, other, outs = refs[:4], refs[4:8], refs[8:12]
    queries, keys, values = refs[12:]
    rows = own[0].shape[0]
    b = rows // 2
    sub = scalars[SUB]
    for s in range(4):
        for c in range(2):
            queries[c, sub, s] = own[s][c * b : (c + 1) * b, :HEAD]
            queries[c, 1 - sub, s] = other[s][c * b : (c + 1) * b, :HEAD]
        for o, ref in enumerate((own[s], other[s])):
            here = pl.ds((s * 2 + o) * rows, rows)
            keys[here, :] = ref[:, HEAD : 2 * HEAD]
            values[here, :] = ref[:, 2 * HEAD :]
    factor = math.log2(math.e) / math.sqrt(HEAD)
    for s, out in enumerate(outs):
        k = turn(scalars, s)
        for a in range(2):
            source = lax.rem(scalars[SEQ] - 2 * sub - a + 4, 4)
            asked = queries[k // 2, lax.rem(k, 2), source]
            scores = lax.dot_general(
                asked, keys[...], (((1,), (1,)), ((), ())), preferred_element_type=F32
            )
            top = jnp.max(scores, axis=1, keepdims=True)
            expw = jnp.exp2((scores - top) * factor)
            denom = jnp.sum(expw, axis=1, keepdims=True)
            numer = dot(expw.astype(BF16), values[...])
            out[a * b : (a + 1) * b, :] = (numer / denom).astype(BF16)


def finish_kernel(scalars, *refs):
    own, other = refs[:4], refs[4:8]
    keep, got, w_own, w_near, w_far, out, mixed, residual = refs[8:]
    sub = scalars[SUB]
    width = keep.shape[1]
    half = 4 * HEAD
    for s in range(4):
        head = turn(scalars, 4 - s)
        mixed[:, at(head * HEAD, HEAD)] = own[s][...]
        place = lax.rem(head + 2 * (1 - sub) + 2, 4)
        mixed[:, at(half + place * HEAD, HEAD)] = other[s][...]
    residual[:, at(sub * width, width)] = keep[...]
    residual[:, at((1 - sub) * width, width)] = got[...]
    shares = dot(mixed[:, :half], w_own[...])
    shares = shares + dot(mixed[:, half : half + 2 * HEAD], w_near[...])
    shares = shares + dot(mixed[:, half + 2 * HEAD :], w_far[...])
    out[...] = (residual[...].astype(F32) + shares).astype(BF16)


def whole(x):
    zeros = (0,) * len(x.shape)
    return pl.BlockSpec(x.shape, lambda *_: zeros)


def struct(shape, dtype=BF16):
    return jax.ShapeDtypeStruct(shape, dtype)


def call(kernel, scalars, args, outs, scratch, flops, far=(), limit=VMEM_LIMIT):
    moved = sum(math.prod(a.shape) * a.dtype.itemsize for a in (*args, *outs))
    return pl.pallas_call(
        kernel,
        out_shape=outs,
        grid_spec=pltpu.PrefetchScalarGridSpec(
            num_scalar_prefetch=1,
            grid=(1,),
            in_specs=[
                pl.BlockSpec(memory_space=pl.ANY) if i in far else whole(a)
                for i, a in enumerate(args)
            ],
            out_specs=[whole(o) for o in outs],
            scratch_shapes=scratch,
        ),
        compiler_params=pltpu.CompilerParams(
            dimension_semantics=("arbitrary",), vmem_limit_bytes=limit
        ),
        cost_estimate=pl.CostEstimate(flops=flops, transcendentals=0, bytes_accessed=moved),
        name=getattr(kernel, "func", kernel).__name__,
    )(scalars, *args)


def after(x, *earlier):
    return lax.optimization_barrier((x, *earlier))[0]


def per_device_fast(seq_in, conv_gain, conv_weight, w_q, w_k, w_v, w_o):
    rows, width = seq_in.shape
    channels = 4 * width
    n = 4
    b = rows // n
    half = rows // 2
    z, mp, sub = (lax.axis_index(a) for a in ("seq", "mp", "sub"))
    place = mp * 2 + sub
    scalars = jnp.stack([place, place ^ 1, place ^ 2, place ^ 3, sub, z]).astype(jnp.int32)
    hidden = pltpu.VMEM((half, channels), BF16)
    hidden_all = pltpu.VMEM((rows, channels), BF16)
    summed = pltpu.VMEM((rows, width), F32)
    blocks = pltpu.VMEM((n, b, width), BF16)
    block = struct((b, width))
    flops = 2 * half * channels * 3 * width
    out_width = w_o.shape[1] // 2
    sems = pltpu.SemaphoreType.DMA((3, SPLIT))

    def load_taps(layer):
        (w,) = call(
            functools.partial(load_taps_kernel, layer),
            scalars,
            (conv_weight,),
            [struct(conv_weight.shape[1:])],
            [sems],
            0,
            far=(0,),
        )
        return w

    edge, middle = call(
        cut_kernel,
        scalars,
        (seq_in,),
        [struct((half, width))] * 2,
        [pltpu.SemaphoreType.DMA((3,))],
        0,
        far=(0,),
    )
    taps = (conv_gain, load_taps(0))
    edge_across = after(swap(edge, "mp"), taps[1])
    middle_across = swap(middle, "mp")
    middle_near = swap(middle, "sub")
    acc, up, down = call(
        first_edge_kernel,
        scalars,
        (edge, swap(edge, "sub"), edge_across, swap(edge_across, "sub"), *taps),
        [struct((n, b, width), F32), struct((b, width)), struct((b, width))],
        [hidden],
        flops,
    )
    lower = lax.ppermute(up, "seq", [(i, i + 1) for i in range(n - 1)])
    upper = lax.ppermute(down, "seq", [(i + 1, i) for i in range(n - 1)])
    middle_across = after(middle_across, acc)
    (partial,) = call(
        first_middle_kernel,
        scalars,
        (middle, middle_near, middle_across, swap(middle_across, "sub"), *taps, acc),
        [struct((n, b, width), F32)],
        [hidden],
        flops,
    )
    dealt = call(
        deal_kernel,
        scalars,
        (partial, lower, upper),
        [block] * n,
        [blocks],
        0,
    )
    dealt = [dealt[0]] + [rotate(dealt[s], s) for s in range(1, n)]

    taps = (conv_gain, load_taps(1))
    early = after(jnp.concatenate(dealt[:2], axis=0), taps[1])
    late = jnp.concatenate(dealt[2:], axis=0)
    next_taps = load_taps(2)
    low, high = call(
        second_kernel,
        scalars,
        (*gather_parts(early, late, under=next_taps), *taps),
        [struct((half, width))] * 2,
        [hidden_all, summed, blocks],
        flops * 2,
    )
    (w_qkv,) = call(
        load_projections_kernel,
        scalars,
        (w_q, w_k, w_v),
        [struct((3, *w_q.shape))],
        [sems],
        0,
        far=(0, 1, 2),
    )
    mine, theirs, *back = call(
        third_kernel,
        scalars,
        (*gather_parts(low, high, under=w_qkv), conv_gain, next_taps),
        [struct((half, width))] * 2 + [block] * n,
        [hidden_all, summed, blocks],
        flops * 2,
    )

    back = [back[0]] + [rotate(back[s], s) for s in range(1, n)]
    keep, give = call(
        sort_kernel, scalars, back, [struct((half, width))] * 2, [blocks], 0
    )

    parts = (mine, swap(theirs, "sub"), swap(mine, "mp"), swap_both(theirs))
    parts, keep = lax.optimization_barrier((parts, keep))
    projected = call(
        project_kernel,
        scalars,
        (*parts, w_qkv),
        [struct((half, 3 * HEAD))] * n,
        [pltpu.VMEM((half, channels), BF16), pltpu.VMEM((n, half, 3 * HEAD), BF16)],
        2 * half * channels * 3 * n * HEAD,
    )
    received = [projected[0]] + [rotate(projected[s], s) for s in range(1, n)]
    got = swap(give, "sub")
    last = projected[0]

    w_o = after(w_o, last)
    half_rows = w_o.shape[0] // 2
    asked = lax.dynamic_slice(
        w_o, (sub * half_rows, (1 - mp) * out_width), (half_rows, out_width)
    )
    w_own = lax.dynamic_slice_in_dim(w_o, mp * out_width, out_width, 1)
    w_near = swap(asked, "mp")
    w_far = swap(w_near, "sub")

    swapped = [swap(x, "sub") for x in received]
    keys = pltpu.VMEM((8 * half, HEAD), BF16)
    attended = call(
        attend_kernel,
        scalars,
        (*received, *swapped),
        [struct((half, HEAD))] * n,
        [pltpu.VMEM((2, 2, n, b, HEAD), BF16), keys, keys],
        4 * half * 4 * 8 * half * HEAD,
    )
    keep, got, w_near, w_far = lax.optimization_barrier(
        (keep, got, w_near, w_far, attended[0])
    )[:4]
    heads = [attended[0]] + [rotate(attended[s], s) for s in range(1, n)]
    others = [swap(x, "mp") for x in heads]
    (out,) = call(
        finish_kernel,
        scalars,
        (*heads, *others, keep, got, w_own, w_near, w_far),
        [struct((half, out_width))],
        [pltpu.VMEM((half, 8 * HEAD), BF16), pltpu.VMEM((half, out_width), BF16)],
        2 * half * 8 * HEAD * out_width,
    )
    return out


def passed_along(x, axis, by):
    devices = lax.axis_size(axis)
    pairs = [(i, i + by) for i in range(devices) if 0 <= i + by < devices]
    return lax.ppermute(x, axis, pairs)


def tower_section(stream_shard, gain_row, weight_taps, dilation):
    rows_here = stream_shard.shape[0]
    gathered = lax.all_gather(stream_shard, ("mp", "sub"), axis=1, tiled=True)
    widened = gathered.astype(jnp.float32)
    normed = (
        widened * lax.rsqrt(jnp.mean(widened * widened, axis=1, keepdims=True) + 1e-06) * gain_row
    )
    hidden = jax.nn.gelu(normed).astype(jnp.bfloat16)
    tap_terms = jnp.einsum("rc,jco->jro", hidden, weight_taps, preferred_element_type=jnp.float32)
    span_rows = min(dilation, rows_here)
    hop_count = max(dilation // rows_here, 1)
    lower_part = passed_along(
        tap_terms[0, rows_here - span_rows :].astype(jnp.bfloat16), "seq", hop_count
    ).astype(jnp.float32)
    upper_part = passed_along(
        tap_terms[2, :span_rows].astype(jnp.bfloat16), "seq", -hop_count
    ).astype(jnp.float32)
    before = jnp.concatenate([lower_part, tap_terms[0, : rows_here - span_rows]], axis=0)
    after = jnp.concatenate([tap_terms[2, span_rows:], upper_part], axis=0)
    return (stream_shard.astype(jnp.float32) + before + tap_terms[1] + after).astype(jnp.bfloat16)


def per_device(seq_in, conv_gain, conv_weight, w_q, w_k, w_v, w_o):
    rows_here = seq_in.shape[0]
    dilations = (BINS_DEV // 4, BINS_DEV, 2 * BINS_DEV)
    stream = seq_in
    for section_index in range(LAYERS):
        stream = tower_section(
            stream, conv_gain[section_index], conv_weight[section_index], dilations[section_index]
        )
    query_rows = rows_here // lax.axis_size("sub")
    mp_width = w_o.shape[1] // lax.axis_size("mp")
    widest = lax.all_gather(stream, ("mp", "sub"), axis=1, tiled=True)
    query_inputs = lax.dynamic_slice_in_dim(
        widest, lax.axis_index("sub") * query_rows, query_rows, 0
    )
    residual_part = lax.dynamic_slice_in_dim(
        query_inputs, lax.axis_index("mp") * mp_width, mp_width, 1
    )
    heads_here = w_q.shape[1] // HEAD
    queries = (
        jnp.dot(query_inputs, w_q, preferred_element_type=jnp.float32)
        .astype(jnp.bfloat16)
        .reshape(query_rows, heads_here, HEAD)
    )
    keys = (
        jnp.dot(query_inputs, w_k, preferred_element_type=jnp.float32)
        .astype(jnp.bfloat16)
        .reshape(query_rows, heads_here, HEAD)
    )
    values = (
        jnp.dot(query_inputs, w_v, preferred_element_type=jnp.float32)
        .astype(jnp.bfloat16)
        .reshape(query_rows, heads_here, HEAD)
    )
    score_scale = 1.0 / math.sqrt(HEAD)
    running_top = jnp.full((heads_here, query_rows), -1e30, jnp.float32)
    running_numer = jnp.zeros((query_rows, heads_here, HEAD), jnp.float32)
    key_rows = lax.all_gather(keys, ("seq", "sub"), axis=0, tiled=True)
    value_rows = lax.all_gather(values, ("seq", "sub"), axis=0, tiled=True)
    scores = (
        jnp.einsum("qhe,khe->hqk", queries, key_rows, preferred_element_type=jnp.float32)
        * score_scale
    )
    new_top = jnp.maximum(running_top, jnp.max(scores, axis=-1))
    expw = jnp.exp(scores - new_top[:, :, None])
    factor = jnp.exp(running_top - new_top)
    new_denom = jnp.sum(expw, axis=-1)
    contrib = jnp.einsum(
        "hqk,khe->qhe", expw.astype(jnp.bfloat16), value_rows, preferred_element_type=jnp.float32
    )
    new_numer = running_numer * factor.T[:, :, None] + contrib
    attended = (
        (new_numer / new_denom.T[:, :, None])
        .astype(jnp.bfloat16)
        .reshape(query_rows, heads_here * HEAD)
    )
    column_weight = lax.all_to_all(w_o, "mp", split_axis=1, concat_axis=0, tiled=True)
    every_head = lax.all_gather(attended, "mp", axis=1, tiled=True)
    shares = jnp.dot(every_head, column_weight, preferred_element_type=jnp.float32)
    return (residual_part.astype(jnp.float32) + shares).astype(jnp.bfloat16)


def solution(mesh):
    placed = (
        P(("groups", "seq"), ("mp", "sub")),
        P(),
        P(None, None, None, ("mp", "sub")),
        P(None, "mp"),
        P(None, "mp"),
        P(None, "mp"),
        P("mp", None),
    )
    sizes = dict(mesh.shape)
    dealt = sizes["seq"] == 4 and sizes["mp"] == 2 and sizes["sub"] == 2
    return jax.shard_map(
        per_device_fast if dealt else per_device,
        mesh=mesh,
        in_specs=placed,
        out_specs=P(("groups", "seq", "sub"), "mp"),
        check_vma=False,
    )
```

```python
import functools
import math

import jax
import jax.numpy as jnp
from jax import lax
from jax.experimental import pallas as pl
from jax.experimental.pallas import tpu as pltpu
from jax.sharding import PartitionSpec as P

HEAD = 128
LAYERS = 3
BINS_DEV = 512
F32 = jnp.float32
BF16 = jnp.bfloat16
VMEM_LIMIT = 16 * 1024 * 1024
SPLIT = 4


def swap(x, axis):
    return lax.ppermute(x, axis, [(0, 1), (1, 0)])


def swap_both(x):
    return lax.ppermute(x, ("mp", "sub"), [(i, 3 - i) for i in range(4)])


def rotate(x, by):
    n = lax.axis_size("seq")
    return lax.ppermute(x, "seq", [(i, (i + by) % n) for i in range(n)])


def gather_parts(*pieces, under=None):
    across = [swap(x, "mp") for x in pieces]
    if under is not None:
        across = lax.optimization_barrier((across, under))[0]
    near = [swap(x, "sub") for x in pieces]
    return (*pieces, *near, *across, *[swap(x, "sub") for x in across])


def dot(a, b):
    return jnp.dot(a, b, preferred_element_type=F32)


def at(start, size):
    return pl.ds(pl.multiple_of(start, size), size)


SUB, SEQ, MP = 4, 5, 6


def fill_hidden(scalars, parts, gains, layer, hidden, order=None):
    count = len(parts) // 4
    rows, width = parts[0].shape
    quarter = rows * count // 4
    tile = 16
    columns = [at(scalars[p] * width, width) for p in range(4)]
    gain = [gains[layer : layer + 1, c] for c in columns]
    for r in range(0, rows * count, tile):
        here = slice(r % rows, r % rows + tile)
        wide = [parts[p * count + r // rows][here, :].astype(F32) for p in range(4)]
        squares = wide[0] * wide[0]
        for x in wide[1:]:
            squares = squares + x * x
        mean = jnp.sum(squares, axis=1, keepdims=True) / (4 * width)
        scale = lax.rsqrt(mean + 1e-06)
        if order is None:
            target = pl.ds(r, tile)
        else:
            target = at(order[r // quarter] * quarter + r % quarter, tile)
        for p, x in enumerate(wide):
            hidden[target, columns[p]] = jax.nn.gelu(x * scale * gain[p]).astype(BF16)


def turn(scalars, by):
    return lax.rem(scalars[SEQ] + by, 4)


def bring(copies):
    copies = [pltpu.make_async_copy(*copy) for copy in copies]
    for copy in copies:
        copy.start()
    for copy in copies:
        copy.wait()


def load_taps_kernel(layer, scalars, w, gains, out, gains_out, sems):
    size = out.shape[1] // SPLIT
    copies = [(gains, gains_out, sems.at[3, 0])]
    for tap in range(3):
        for i in range(SPLIT):
            rows = pl.ds(i * size, size)
            copies.append((w.at[layer, tap, rows], out.at[tap, rows], sems.at[tap, i]))
    bring(copies)


def load_projections_kernel(scalars, w_q, w_k, w_v, w_o, out, own, asked, sems):
    size = out.shape[1] // SPLIT
    copies = []
    for m, w in enumerate((w_q, w_k, w_v)):
        for i in range(SPLIT):
            rows = pl.ds(i * size, size)
            copies.append((w.at[rows], out.at[m, rows], sems.at[m, i]))
    half, width = asked.shape
    mp = scalars[MP]
    copies.append((w_o.at[:, at(mp * width, width)], own, sems.at[3, 0]))
    rows = at(scalars[SUB] * half, half)
    copies.append((w_o.at[rows, at((1 - mp) * width, width)], asked, sems.at[3, 1]))
    bring(copies)


def cut_kernel(scalars, x, edge, middle, sems):
    b = edge.shape[0] // 2
    bring(
        [
            (x.at[pl.ds(0, b)], edge.at[pl.ds(0, b)], sems.at[0]),
            (x.at[pl.ds(3 * b, b)], edge.at[pl.ds(b, b)], sems.at[1]),
            (x.at[pl.ds(b, 2 * b)], middle, sems.at[2]),
        ]
    )


def first_edge_kernel(scalars, p0, p1, p2, p3, gains, w, acc, outer, inner, hidden):
    fill_hidden(scalars, (p0, p1, p2, p3), gains, 0, hidden)
    b = outer.shape[0]
    middle = p0[...].astype(F32) + dot(hidden[...], w[1])
    before = dot(hidden[...], w[0])
    after = dot(hidden[...], w[2])
    odd = lax.rem(scalars[SEQ], 2) == 1
    up, down = before[b:], after[:b]
    outer[...] = jnp.where(odd, down, up).astype(BF16)
    inner[...] = jnp.where(odd, up, down).astype(BF16)
    acc[0] = middle[:b]
    acc[1] = before[:b]
    acc[2] = after[b:]
    acc[3] = middle[b:]


def first_middle_kernel(
    scalars, p0, p1, p2, p3, gains, w, acc, partial, hidden
):
    fill_hidden(scalars, (p0, p1, p2, p3), gains, 0, hidden)
    b = acc.shape[1]
    middle = p0[...].astype(F32) + dot(hidden[...], w[1])
    before = dot(hidden[...], w[0])
    after = dot(hidden[...], w[2])
    partial[0] = acc[0] + after[:b]
    partial[1] = acc[1] + middle[:b] + after[b:]
    partial[2] = acc[2] + middle[b:] + before[:b]
    partial[3] = acc[3] + before[b:]


def deal_kernel(scalars, partial, outer, inner, *refs):
    outs, stream = refs[:4], refs[4]
    odd = lax.rem(scalars[SEQ], 2) == 1
    from_outer, from_inner = outer[...].astype(F32), inner[...].astype(F32)
    lower = jnp.where(odd, from_outer, from_inner)
    upper = jnp.where(odd, from_inner, from_outer)
    stream[0] = (partial[0] + lower).astype(BF16)
    stream[1] = partial[1].astype(BF16)
    stream[2] = partial[2].astype(BF16)
    stream[3] = (partial[3] + upper).astype(BF16)
    for s, out in enumerate(outs):
        out[...] = stream[turn(scalars, s)]


def local_taps(hidden, acc, w, shift):
    rows = hidden.shape[0]
    acc[...] = dot(hidden[...], w[1])
    acc[shift:, :] += dot(hidden[: rows - shift, :], w[0])
    acc[: rows - shift, :] += dot(hidden[shift:, :], w[2])


def second_kernel(scalars, *refs):
    parts = refs[:8]
    gains, w, low, high, hidden, acc, kept = refs[8:]
    half = low.shape[0]
    b = half // 2
    order = [turn(scalars, 4 - s) for s in range(4)]
    fill_hidden(scalars, parts, gains, 1, hidden, order)
    for s in range(4):
        kept[order[s]] = parts[s // 2][(s % 2) * b : (s % 2 + 1) * b, :]
    local_taps(hidden, acc, w, b)
    for k in range(4):
        out = low if k < 2 else high
        made = kept[k].astype(F32) + acc[k * b : (k + 1) * b, :]
        out[(k % 2) * b : (k % 2 + 1) * b, :] = made.astype(BF16)


def third_kernel(scalars, *refs):
    parts = refs[:8]
    gains, w = refs[8:10]
    mine, theirs = refs[10:12]
    outs = refs[12:16]
    hidden, acc, made = refs[16:]
    half = parts[0].shape[0]
    b = half // 2
    fill_hidden(scalars, parts, gains, 2, hidden)
    local_taps(hidden, acc, w, half)
    for k in range(4):
        own = parts[k // 2][(k % 2) * b : (k % 2 + 1) * b, :].astype(F32)
        made[k] = (own + acc[k * b : (k + 1) * b, :]).astype(BF16)
    sub = scalars[SUB]
    for c in range(2):
        rows = slice(c * b, (c + 1) * b)
        mine[rows, :] = made[2 * c + sub]
        theirs[rows, :] = made[2 * c + 1 - sub]
    for s, out in enumerate(outs):
        out[...] = made[turn(scalars, s)]


def project_kernel(scalars, p0, p1, p2, p3, w, o0, o1, o2, o3, rows, made):
    width = p0.shape[1]
    for p, part in enumerate((p0, p1, p2, p3)):
        rows[:, at(scalars[p] * width, width)] = part[...]
    for i in range(3):
        product = dot(rows[...], w[i]).astype(BF16)
        for h in range(4):
            made[h, :, i * HEAD : (i + 1) * HEAD] = product[:, h * HEAD : (h + 1) * HEAD]
    for s, out in enumerate((o0, o1, o2, o3)):
        out[...] = made[turn(scalars, s)]


def attend_kernel(scalars, *refs):
    own, other, arrived, outs = refs[:4], refs[4:8], refs[8:12], refs[12:16]
    keep, give, queries, keys, values, ordered = refs[16:]
    b = own[0].shape[0] // 2
    sub = scalars[SUB]
    for s in range(4):
        ordered[turn(scalars, 4 - s)] = arrived[s][...]
    for a in range(2):
        rows = slice(a * b, (a + 1) * b)
        keep[rows, :] = ordered[2 * sub + a]
        give[rows, :] = ordered[2 * (1 - sub) + a]
    rows = own[0].shape[0]
    for s in range(4):
        for c in range(2):
            queries[c, sub, s] = own[s][c * b : (c + 1) * b, :HEAD]
            queries[c, 1 - sub, s] = other[s][c * b : (c + 1) * b, :HEAD]
        for o, ref in enumerate((own[s], other[s])):
            here = pl.ds((s * 2 + o) * rows, rows)
            keys[here, :] = ref[:, HEAD : 2 * HEAD]
            values[here, :] = ref[:, 2 * HEAD :]
    factor = math.log2(math.e) / math.sqrt(HEAD)
    for s, out in enumerate(outs):
        k = turn(scalars, s)
        for a in range(2):
            source = lax.rem(scalars[SEQ] - 2 * sub - a + 4, 4)
            asked = queries[k // 2, lax.rem(k, 2), source]
            scores = lax.dot_general(
                asked, keys[...], (((1,), (1,)), ((), ())), preferred_element_type=F32
            )
            top = jnp.max(scores, axis=1, keepdims=True)
            expw = jnp.exp2((scores - top) * factor)
            denom = jnp.sum(expw, axis=1, keepdims=True)
            numer = dot(expw.astype(BF16), values[...])
            out[a * b : (a + 1) * b, :] = (numer / denom).astype(BF16)


def finish_kernel(scalars, *refs):
    own, other = refs[:4], refs[4:8]
    keep, got, w_own, w_near, w_far, out, mixed, residual = refs[8:]
    sub = scalars[SUB]
    width = keep.shape[1]
    half = 4 * HEAD
    for s in range(4):
        head = turn(scalars, 4 - s)
        mixed[:, at(head * HEAD, HEAD)] = own[s][...]
        place = lax.rem(head + 2 * (1 - sub) + 2, 4)
        mixed[:, at(half + place * HEAD, HEAD)] = other[s][...]
    residual[:, at(sub * width, width)] = keep[...]
    residual[:, at((1 - sub) * width, width)] = got[...]
    shares = dot(mixed[:, :half], w_own[...])
    shares = shares + dot(mixed[:, half : half + 2 * HEAD], w_near[...])
    shares = shares + dot(mixed[:, half + 2 * HEAD :], w_far[...])
    out[...] = (residual[...].astype(F32) + shares).astype(BF16)


def whole(x):
    zeros = (0,) * len(x.shape)
    return pl.BlockSpec(x.shape, lambda *_: zeros)


def struct(shape, dtype=BF16):
    return jax.ShapeDtypeStruct(shape, dtype)


def call(kernel, scalars, args, outs, scratch, flops, far=(), limit=VMEM_LIMIT):
    moved = sum(math.prod(a.shape) * a.dtype.itemsize for a in (*args, *outs))
    return pl.pallas_call(
        kernel,
        out_shape=outs,
        grid_spec=pltpu.PrefetchScalarGridSpec(
            num_scalar_prefetch=1,
            grid=(1,),
            in_specs=[
                pl.BlockSpec(memory_space=pltpu.HBM) if i in far else whole(a)
                for i, a in enumerate(args)
            ],
            out_specs=[whole(o) for o in outs],
            scratch_shapes=scratch,
        ),
        compiler_params=pltpu.CompilerParams(
            dimension_semantics=("arbitrary",), vmem_limit_bytes=limit
        ),
        cost_estimate=pl.CostEstimate(flops=flops, transcendentals=0, bytes_accessed=moved),
        name=getattr(kernel, "func", kernel).__name__,
    )(scalars, *args)


def after(x, *earlier):
    return lax.optimization_barrier((x, *earlier))[0]


def per_device_fast(seq_in, conv_gain, conv_weight, w_q, w_k, w_v, w_o):
    seq_in, conv_gain, conv_weight, w_q, w_k, w_v, w_o = (
        pltpu.with_memory_space_constraint(w, pltpu.HBM)
        for w in (seq_in, conv_gain, conv_weight, w_q, w_k, w_v, w_o)
    )
    rows, width = seq_in.shape
    channels = 4 * width
    n = 4
    b = rows // n
    half = rows // 2
    z, mp, sub = (lax.axis_index(a) for a in ("seq", "mp", "sub"))
    place = mp * 2 + sub
    scalars = jnp.stack([place, place ^ 1, place ^ 2, place ^ 3, sub, z, mp]).astype(jnp.int32)
    hidden = pltpu.VMEM((half, channels), BF16)
    hidden_all = pltpu.VMEM((rows, channels), BF16)
    summed = pltpu.VMEM((rows, width), F32)
    blocks = pltpu.VMEM((n, b, width), BF16)
    block = struct((b, width))
    flops = 2 * half * channels * 3 * width
    out_width = w_o.shape[1] // 2
    sems = pltpu.SemaphoreType.DMA((4, SPLIT))

    def load_taps(layer):
        w, gains = call(
            functools.partial(load_taps_kernel, layer),
            scalars,
            (conv_weight, conv_gain),
            [struct(conv_weight.shape[1:]), struct(conv_gain.shape, F32)],
            [sems],
            0,
            far=(0, 1),
        )
        return gains, w

    edge, middle = call(
        cut_kernel,
        scalars,
        (seq_in,),
        [struct((half, width))] * 2,
        [pltpu.SemaphoreType.DMA((3,))],
        0,
        far=(0,),
    )
    taps = load_taps(0)
    edge_across, middle_across = after(swap(edge, "mp"), taps[1]), swap(middle, "mp")
    acc, outer, inner = call(
        first_edge_kernel,
        scalars,
        (edge, swap(edge, "sub"), edge_across, swap(edge_across, "sub"), *taps),
        [struct((n, b, width), F32), block, block],
        [hidden],
        flops,
    )
    outer = lax.ppermute(outer, "seq", [(i, i ^ 1) for i in range(n)])
    inner = lax.ppermute(inner, "seq", [(1, 2), (2, 1)])
    middle_near = swap(middle, "sub")
    (partial,) = call(
        first_middle_kernel,
        scalars,
        (middle, middle_near, middle_across, swap(middle_across, "sub"), *taps, acc),
        [struct((n, b, width), F32)],
        [hidden],
        flops,
    )
    dealt = call(
        deal_kernel,
        scalars,
        (partial, outer, inner),
        [block] * n,
        [blocks],
        0,
    )
    dealt = [dealt[0]] + [rotate(dealt[s], s) for s in range(1, n)]

    taps = load_taps(1)
    early = jnp.concatenate(dealt[:2], axis=0)
    late = jnp.concatenate(dealt[2:], axis=0)
    low, high = call(
        second_kernel,
        scalars,
        (*gather_parts(early, late, under=taps[1]), *taps),
        [struct((half, width))] * 2,
        [hidden_all, summed, blocks],
        flops * 2,
    )
    w_qkv, w_own, asked = call(
        load_projections_kernel,
        scalars,
        (w_q, w_k, w_v, w_o),
        [
            struct((3, *w_q.shape)),
            struct((w_o.shape[0], out_width)),
            struct((w_o.shape[0] // 2, out_width)),
        ],
        [sems],
        0,
        far=(0, 1, 2, 3),
    )
    taps = load_taps(2)
    mine, theirs, *back = call(
        third_kernel,
        scalars,
        (*gather_parts(low, high, under=(taps[1], w_qkv)), *taps),
        [struct((half, width))] * 2 + [block] * n,
        [hidden_all, summed, blocks],
        flops * 2,
    )

    near = swap(theirs, "sub")
    back = [after(x, near) for x in back]
    back = [back[0]] + [rotate(back[s], s) for s in range(1, n)]
    parts = (mine, near, swap(mine, "mp"), swap_both(theirs))
    projected = call(
        project_kernel,
        scalars,
        (*parts, w_qkv),
        [struct((half, 3 * HEAD))] * n,
        [pltpu.VMEM((half, channels), BF16), pltpu.VMEM((n, half, 3 * HEAD), BF16)],
        2 * half * channels * 3 * n * HEAD,
    )
    projected, back = lax.optimization_barrier((projected, back))
    received = [projected[0]] + [rotate(projected[s], s) for s in range(1, n)]
    asked = after(asked, back[1])
    w_near = swap(asked, "mp")
    w_far = swap(w_near, "sub")

    swapped = [swap(x, "sub") for x in received]
    keys = pltpu.VMEM((8 * half, HEAD), BF16)
    *attended, keep, give = call(
        attend_kernel,
        scalars,
        (*received, *swapped, *back),
        [struct((half, HEAD))] * n + [struct((half, width))] * 2,
        [pltpu.VMEM((2, 2, n, b, HEAD), BF16), keys, keys, blocks],
        4 * half * 4 * 8 * half * HEAD,
    )
    got = swap(give, "sub")
    heads = [attended[0]] + [rotate(attended[s], s) for s in range(1, n)]
    others = [swap(x, "mp") for x in heads]
    (out,) = call(
        finish_kernel,
        scalars,
        (*heads, *others, keep, got, w_own, w_near, w_far),
        [struct((half, out_width))],
        [pltpu.VMEM((half, 8 * HEAD), BF16), pltpu.VMEM((half, out_width), BF16)],
        2 * half * 8 * HEAD * out_width,
    )
    return out


def passed_along(x, axis, by):
    devices = lax.axis_size(axis)
    pairs = [(i, i + by) for i in range(devices) if 0 <= i + by < devices]
    return lax.ppermute(x, axis, pairs)


def tower_section(stream_shard, gain_row, weight_taps, dilation):
    rows_here = stream_shard.shape[0]
    gathered = lax.all_gather(stream_shard, ("mp", "sub"), axis=1, tiled=True)
    widened = gathered.astype(jnp.float32)
    normed = (
        widened * lax.rsqrt(jnp.mean(widened * widened, axis=1, keepdims=True) + 1e-06) * gain_row
    )
    hidden = jax.nn.gelu(normed).astype(jnp.bfloat16)
    tap_terms = jnp.einsum("rc,jco->jro", hidden, weight_taps, preferred_element_type=jnp.float32)
    span_rows = min(dilation, rows_here)
    hop_count = max(dilation // rows_here, 1)
    lower_part = passed_along(
        tap_terms[0, rows_here - span_rows :].astype(jnp.bfloat16), "seq", hop_count
    ).astype(jnp.float32)
    upper_part = passed_along(
        tap_terms[2, :span_rows].astype(jnp.bfloat16), "seq", -hop_count
    ).astype(jnp.float32)
    before = jnp.concatenate([lower_part, tap_terms[0, : rows_here - span_rows]], axis=0)
    after = jnp.concatenate([tap_terms[2, span_rows:], upper_part], axis=0)
    return (stream_shard.astype(jnp.float32) + before + tap_terms[1] + after).astype(jnp.bfloat16)


def per_device(seq_in, conv_gain, conv_weight, w_q, w_k, w_v, w_o):
    rows_here = seq_in.shape[0]
    dilations = (BINS_DEV // 4, BINS_DEV, 2 * BINS_DEV)
    stream = seq_in
    for section_index in range(LAYERS):
        stream = tower_section(
            stream, conv_gain[section_index], conv_weight[section_index], dilations[section_index]
        )
    query_rows = rows_here // lax.axis_size("sub")
    mp_width = w_o.shape[1] // lax.axis_size("mp")
    widest = lax.all_gather(stream, ("mp", "sub"), axis=1, tiled=True)
    query_inputs = lax.dynamic_slice_in_dim(
        widest, lax.axis_index("sub") * query_rows, query_rows, 0
    )
    residual_part = lax.dynamic_slice_in_dim(
        query_inputs, lax.axis_index("mp") * mp_width, mp_width, 1
    )
    heads_here = w_q.shape[1] // HEAD
    queries = (
        jnp.dot(query_inputs, w_q, preferred_element_type=jnp.float32)
        .astype(jnp.bfloat16)
        .reshape(query_rows, heads_here, HEAD)
    )
    keys = (
        jnp.dot(query_inputs, w_k, preferred_element_type=jnp.float32)
        .astype(jnp.bfloat16)
        .reshape(query_rows, heads_here, HEAD)
    )
    values = (
        jnp.dot(query_inputs, w_v, preferred_element_type=jnp.float32)
        .astype(jnp.bfloat16)
        .reshape(query_rows, heads_here, HEAD)
    )
    score_scale = 1.0 / math.sqrt(HEAD)
    running_top = jnp.full((heads_here, query_rows), -1e30, jnp.float32)
    running_numer = jnp.zeros((query_rows, heads_here, HEAD), jnp.float32)
    key_rows = lax.all_gather(keys, ("seq", "sub"), axis=0, tiled=True)
    value_rows = lax.all_gather(values, ("seq", "sub"), axis=0, tiled=True)
    scores = (
        jnp.einsum("qhe,khe->hqk", queries, key_rows, preferred_element_type=jnp.float32)
        * score_scale
    )
    new_top = jnp.maximum(running_top, jnp.max(scores, axis=-1))
    expw = jnp.exp(scores - new_top[:, :, None])
    factor = jnp.exp(running_top - new_top)
    new_denom = jnp.sum(expw, axis=-1)
    contrib = jnp.einsum(
        "hqk,khe->qhe", expw.astype(jnp.bfloat16), value_rows, preferred_element_type=jnp.float32
    )
    new_numer = running_numer * factor.T[:, :, None] + contrib
    attended = (
        (new_numer / new_denom.T[:, :, None])
        .astype(jnp.bfloat16)
        .reshape(query_rows, heads_here * HEAD)
    )
    column_weight = lax.all_to_all(w_o, "mp", split_axis=1, concat_axis=0, tiled=True)
    every_head = lax.all_gather(attended, "mp", axis=1, tiled=True)
    shares = jnp.dot(every_head, column_weight, preferred_element_type=jnp.float32)
    return (residual_part.astype(jnp.float32) + shares).astype(jnp.bfloat16)


def solution(mesh):
    placed = (
        P(("groups", "seq"), ("mp", "sub")),
        P(),
        P(None, None, None, ("mp", "sub")),
        P(None, "mp"),
        P(None, "mp"),
        P(None, "mp"),
        P("mp", None),
    )
    sizes = dict(mesh.shape)
    dealt = sizes["seq"] == 4 and sizes["mp"] == 2 and sizes["sub"] == 2
    return jax.shard_map(
        per_device_fast if dealt else per_device,
        mesh=mesh,
        in_specs=placed,
        out_specs=P(("groups", "seq", "sub"), "mp"),
        check_vma=False,
    )
```

```python
import functools
import math

import jax
import jax.numpy as jnp
from jax import lax
from jax.experimental import pallas as pl
from jax.experimental.pallas import tpu as pltpu
from jax.sharding import PartitionSpec as P

HEAD = 128
LAYERS = 3
BINS_DEV = 512
F32 = jnp.float32
BF16 = jnp.bfloat16
VMEM_LIMIT = 16 * 1024 * 1024
SPLIT = 4


def swap(x, axis):
    return lax.ppermute(x, axis, [(0, 1), (1, 0)])


def swap_both(x):
    return lax.ppermute(x, ("mp", "sub"), [(i, 3 - i) for i in range(4)])


def rotate(x, by):
    n = lax.axis_size("seq")
    return lax.ppermute(x, "seq", [(i, (i + by) % n) for i in range(n)])


def gather_parts(*pieces, under=None):
    across = [swap(x, "mp") for x in pieces]
    if under is not None:
        across = lax.optimization_barrier((across, under))[0]
    near = [swap(x, "sub") for x in pieces]
    return (*pieces, *near, *across, *[swap(x, "sub") for x in across])


def dot(a, b):
    return jnp.dot(a, b, preferred_element_type=F32)


def at(start, size):
    return pl.ds(pl.multiple_of(start, size), size)


SUB, SEQ, MP = 4, 5, 6


def fill_hidden(scalars, parts, gains, layer, hidden, order=None):
    count = len(parts) // 4
    rows, width = parts[0].shape
    quarter = rows * count // 4
    tile = 16
    columns = [at(scalars[p] * width, width) for p in range(4)]
    gain = [gains[layer : layer + 1, c] for c in columns]
    for r in range(0, rows * count, tile):
        here = slice(r % rows, r % rows + tile)
        wide = [parts[p * count + r // rows][here, :].astype(F32) for p in range(4)]
        squares = wide[0] * wide[0]
        for x in wide[1:]:
            squares = squares + x * x
        mean = jnp.sum(squares, axis=1, keepdims=True) / (4 * width)
        scale = lax.rsqrt(mean + 1e-06)
        if order is None:
            target = pl.ds(r, tile)
        else:
            target = at(order[r // quarter] * quarter + r % quarter, tile)
        for p, x in enumerate(wide):
            hidden[target, columns[p]] = jax.nn.gelu(x * scale * gain[p]).astype(BF16)


def turn(scalars, by):
    return lax.rem(scalars[SEQ] + by, 4)


def bring(copies):
    copies = [pltpu.make_async_copy(*copy) for copy in copies]
    for copy in copies:
        copy.start()
    for copy in copies:
        copy.wait()


def load_taps_kernel(layer, scalars, w, gains, out, gains_out, sems):
    size = out.shape[1] // SPLIT
    copies = [(gains, gains_out, sems.at[3, 0])]
    for tap in range(3):
        for i in range(SPLIT):
            rows = pl.ds(i * size, size)
            copies.append((w.at[layer, tap, rows], out.at[tap, rows], sems.at[tap, i]))
    bring(copies)


def load_projections_kernel(scalars, w_q, w_k, w_v, w_o, out, own, asked, sems):
    size = out.shape[1] // SPLIT
    copies = []
    for m, w in enumerate((w_q, w_k, w_v)):
        for i in range(SPLIT):
            rows = pl.ds(i * size, size)
            copies.append((w.at[rows], out.at[m, rows], sems.at[m, i]))
    half, width = asked.shape
    mp = scalars[MP]
    copies.append((w_o.at[:, at(mp * width, width)], own, sems.at[3, 0]))
    rows = at(scalars[SUB] * half, half)
    copies.append((w_o.at[rows, at((1 - mp) * width, width)], asked, sems.at[3, 1]))
    bring(copies)


def cut_kernel(scalars, x, edge, middle, sems):
    b = edge.shape[0] // 2
    size = 2 * b // SPLIT
    copies = []
    for i in range(SPLIT):
        rows = pl.ds(i * size, size)
        start = i * size if i * size < b else i * size + 2 * b
        copies.append((x.at[pl.ds(start, size)], edge.at[rows], sems.at[0, i]))
        copies.append((x.at[pl.ds(b + i * size, size)], middle.at[rows], sems.at[1, i]))
    bring(copies)


def first_edge_kernel(scalars, p0, p1, p2, p3, gains, w, acc, outer, inner, hidden):
    fill_hidden(scalars, (p0, p1, p2, p3), gains, 0, hidden)
    b = outer.shape[0]
    middle = p0[...].astype(F32) + dot(hidden[...], w[1])
    before = dot(hidden[...], w[0])
    after = dot(hidden[...], w[2])
    odd = lax.rem(scalars[SEQ], 2) == 1
    up, down = before[b:], after[:b]
    outer[...] = jnp.where(odd, down, up).astype(BF16)
    inner[...] = jnp.where(odd, up, down).astype(BF16)
    acc[0] = middle[:b]
    acc[1] = before[:b]
    acc[2] = after[b:]
    acc[3] = middle[b:]


def first_middle_kernel(
    scalars, p0, p1, p2, p3, gains, w, acc, partial, hidden
):
    fill_hidden(scalars, (p0, p1, p2, p3), gains, 0, hidden)
    b = acc.shape[1]
    middle = p0[...].astype(F32) + dot(hidden[...], w[1])
    before = dot(hidden[...], w[0])
    after = dot(hidden[...], w[2])
    partial[0] = acc[0] + after[:b]
    partial[1] = acc[1] + middle[:b] + after[b:]
    partial[2] = acc[2] + middle[b:] + before[:b]
    partial[3] = acc[3] + before[b:]


def deal_kernel(scalars, partial, outer, inner, *refs):
    outs, stream = refs[:4], refs[4]
    odd = lax.rem(scalars[SEQ], 2) == 1
    from_outer, from_inner = outer[...].astype(F32), inner[...].astype(F32)
    lower = jnp.where(odd, from_outer, from_inner)
    upper = jnp.where(odd, from_inner, from_outer)
    stream[0] = (partial[0] + lower).astype(BF16)
    stream[1] = partial[1].astype(BF16)
    stream[2] = partial[2].astype(BF16)
    stream[3] = (partial[3] + upper).astype(BF16)
    for s, out in enumerate(outs):
        out[...] = stream[turn(scalars, s)]


def local_taps(hidden, acc, w, shift):
    rows = hidden.shape[0]
    acc[...] = dot(hidden[...], w[1])
    acc[shift:, :] += dot(hidden[: rows - shift, :], w[0])
    acc[: rows - shift, :] += dot(hidden[shift:, :], w[2])


def second_kernel(scalars, *refs):
    parts = refs[:8]
    gains, w, low, high, hidden, acc, kept = refs[8:]
    half = low.shape[0]
    b = half // 2
    order = [turn(scalars, 4 - s) for s in range(4)]
    fill_hidden(scalars, parts, gains, 1, hidden, order)
    for s in range(4):
        kept[order[s]] = parts[s // 2][(s % 2) * b : (s % 2 + 1) * b, :]
    local_taps(hidden, acc, w, b)
    for k in range(4):
        out = low if k < 2 else high
        made = kept[k].astype(F32) + acc[k * b : (k + 1) * b, :]
        out[(k % 2) * b : (k % 2 + 1) * b, :] = made.astype(BF16)


def third_kernel(scalars, *refs):
    parts = refs[:8]
    gains, w = refs[8:10]
    mine, theirs = refs[10:12]
    outs = refs[12:16]
    hidden, acc, made = refs[16:]
    half = parts[0].shape[0]
    b = half // 2
    fill_hidden(scalars, parts, gains, 2, hidden)
    local_taps(hidden, acc, w, half)
    for k in range(4):
        own = parts[k // 2][(k % 2) * b : (k % 2 + 1) * b, :].astype(F32)
        made[k] = (own + acc[k * b : (k + 1) * b, :]).astype(BF16)
    sub = scalars[SUB]
    for c in range(2):
        rows = slice(c * b, (c + 1) * b)
        mine[rows, :] = made[2 * c + sub]
        theirs[rows, :] = made[2 * c + 1 - sub]
    for s, out in enumerate(outs):
        out[...] = made[turn(scalars, s)]


def project_kernel(scalars, p0, p1, p2, p3, w, o0, o1, o2, o3, rows, made):
    width = p0.shape[1]
    for p, part in enumerate((p0, p1, p2, p3)):
        rows[:, at(scalars[p] * width, width)] = part[...]
    for i in range(3):
        product = dot(rows[...], w[i]).astype(BF16)
        for h in range(4):
            made[h, :, i * HEAD : (i + 1) * HEAD] = product[:, h * HEAD : (h + 1) * HEAD]
    for s, out in enumerate((o0, o1, o2, o3)):
        out[...] = made[turn(scalars, s)]


def attend_kernel(scalars, *refs):
    own, other, arrived, outs = refs[:4], refs[4:8], refs[8:12], refs[12:16]
    keep, give, queries, keys, values, ordered = refs[16:]
    b = own[0].shape[0] // 2
    sub = scalars[SUB]
    for s in range(4):
        ordered[turn(scalars, 4 - s)] = arrived[s][...]
    for a in range(2):
        rows = slice(a * b, (a + 1) * b)
        keep[rows, :] = ordered[2 * sub + a]
        give[rows, :] = ordered[2 * (1 - sub) + a]
    rows = own[0].shape[0]
    for s in range(4):
        for c in range(2):
            queries[c, sub, s] = own[s][c * b : (c + 1) * b, :HEAD]
            queries[c, 1 - sub, s] = other[s][c * b : (c + 1) * b, :HEAD]
        for o, ref in enumerate((own[s], other[s])):
            here = pl.ds((s * 2 + o) * rows, rows)
            keys[here, :] = ref[:, HEAD : 2 * HEAD]
            values[here, :] = ref[:, 2 * HEAD :]
    factor = math.log2(math.e) / math.sqrt(HEAD)
    for s, out in enumerate(outs):
        k = turn(scalars, s)
        asked = jnp.concatenate(
            [
                queries[k // 2, lax.rem(k, 2), lax.rem(scalars[SEQ] - 2 * sub - a + 4, 4)]
                for a in range(2)
            ],
            axis=0,
        )
        scores = lax.dot_general(
            asked, keys[...], (((1,), (1,)), ((), ())), preferred_element_type=F32
        )
        top = jnp.max(scores, axis=1, keepdims=True)
        expw = jnp.exp2((scores - top) * factor)
        denom = jnp.sum(expw, axis=1, keepdims=True)
        numer = dot(expw.astype(BF16), values[...])
        out[...] = (numer / denom).astype(BF16)


def finish_kernel(scalars, *refs):
    own, other = refs[:4], refs[4:8]
    keep, got, w_own, w_near, w_far, out, mixed, residual = refs[8:]
    sub = scalars[SUB]
    width = keep.shape[1]
    half = 4 * HEAD
    for s in range(4):
        head = turn(scalars, 4 - s)
        mixed[:, at(head * HEAD, HEAD)] = own[s][...]
        place = lax.rem(head + 2 * (1 - sub) + 2, 4)
        mixed[:, at(half + place * HEAD, HEAD)] = other[s][...]
    residual[:, at(sub * width, width)] = keep[...]
    residual[:, at((1 - sub) * width, width)] = got[...]
    shares = dot(mixed[:, :half], w_own[...])
    shares = shares + dot(mixed[:, half : half + 2 * HEAD], w_near[...])
    shares = shares + dot(mixed[:, half + 2 * HEAD :], w_far[...])
    out[...] = (residual[...].astype(F32) + shares).astype(BF16)


def whole(x):
    zeros = (0,) * len(x.shape)
    return pl.BlockSpec(x.shape, lambda *_: zeros)


def struct(shape, dtype=BF16):
    return jax.ShapeDtypeStruct(shape, dtype)


def call(kernel, scalars, args, outs, scratch, flops, far=(), limit=VMEM_LIMIT):
    moved = sum(math.prod(a.shape) * a.dtype.itemsize for a in (*args, *outs))
    return pl.pallas_call(
        kernel,
        out_shape=outs,
        grid_spec=pltpu.PrefetchScalarGridSpec(
            num_scalar_prefetch=1,
            grid=(1,),
            in_specs=[
                pl.BlockSpec(memory_space=pltpu.HBM) if i in far else whole(a)
                for i, a in enumerate(args)
            ],
            out_specs=[whole(o) for o in outs],
            scratch_shapes=scratch,
        ),
        compiler_params=pltpu.CompilerParams(
            dimension_semantics=("arbitrary",), vmem_limit_bytes=limit
        ),
        cost_estimate=pl.CostEstimate(flops=flops, transcendentals=0, bytes_accessed=moved),
        name=getattr(kernel, "func", kernel).__name__,
    )(scalars, *args)


def after(x, *earlier):
    return lax.optimization_barrier((x, *earlier))[0]


def per_device_fast(seq_in, conv_gain, conv_weight, w_q, w_k, w_v, w_o):
    seq_in, conv_gain, conv_weight, w_q, w_k, w_v, w_o = (
        pltpu.with_memory_space_constraint(w, pltpu.HBM)
        for w in (seq_in, conv_gain, conv_weight, w_q, w_k, w_v, w_o)
    )
    rows, width = seq_in.shape
    channels = 4 * width
    n = 4
    b = rows // n
    half = rows // 2
    z, mp, sub = (lax.axis_index(a) for a in ("seq", "mp", "sub"))
    place = mp * 2 + sub
    scalars = jnp.stack([place, place ^ 1, place ^ 2, place ^ 3, sub, z, mp]).astype(jnp.int32)
    hidden = pltpu.VMEM((half, channels), BF16)
    hidden_all = pltpu.VMEM((rows, channels), BF16)
    summed = pltpu.VMEM((rows, width), F32)
    blocks = pltpu.VMEM((n, b, width), BF16)
    block = struct((b, width))
    flops = 2 * half * channels * 3 * width
    out_width = w_o.shape[1] // 2
    sems = pltpu.SemaphoreType.DMA((4, SPLIT))

    def load_taps(layer):
        w, gains = call(
            functools.partial(load_taps_kernel, layer),
            scalars,
            (conv_weight, conv_gain),
            [struct(conv_weight.shape[1:]), struct(conv_gain.shape, F32)],
            [sems],
            0,
            far=(0, 1),
        )
        return gains, w

    edge, middle = call(
        cut_kernel,
        scalars,
        (seq_in,),
        [struct((half, width))] * 2,
        [sems],
        0,
        far=(0,),
    )
    taps = load_taps(0)
    edge_across, middle_across = after(swap(edge, "mp"), taps[1]), swap(middle, "mp")
    acc, outer, inner = call(
        first_edge_kernel,
        scalars,
        (edge, swap(edge, "sub"), edge_across, swap(edge_across, "sub"), *taps),
        [struct((n, b, width), F32), block, block],
        [hidden],
        flops,
    )
    outer = lax.ppermute(outer, "seq", [(i, i ^ 1) for i in range(n)])
    inner = lax.ppermute(inner, "seq", [(1, 2), (2, 1)])
    middle_near = swap(middle, "sub")
    (partial,) = call(
        first_middle_kernel,
        scalars,
        (middle, middle_near, middle_across, swap(middle_across, "sub"), *taps, acc),
        [struct((n, b, width), F32)],
        [hidden],
        flops,
    )
    dealt = call(
        deal_kernel,
        scalars,
        (partial, outer, inner),
        [block] * n,
        [blocks],
        0,
    )
    dealt = [dealt[0]] + [rotate(dealt[s], s) for s in range(1, n)]

    taps = load_taps(1)
    early = jnp.concatenate(dealt[:2], axis=0)
    late = jnp.concatenate(dealt[2:], axis=0)
    low, high = call(
        second_kernel,
        scalars,
        (*gather_parts(early, late, under=taps[1]), *taps),
        [struct((half, width))] * 2,
        [hidden_all, summed, blocks],
        flops * 2,
    )
    w_qkv, w_own, asked = call(
        load_projections_kernel,
        scalars,
        (w_q, w_k, w_v, w_o),
        [
            struct((3, *w_q.shape)),
            struct((w_o.shape[0], out_width)),
            struct((w_o.shape[0] // 2, out_width)),
        ],
        [sems],
        0,
        far=(0, 1, 2, 3),
    )
    taps = load_taps(2)
    mine, theirs, *back = call(
        third_kernel,
        scalars,
        (*gather_parts(low, high, under=(taps[1], w_qkv)), *taps),
        [struct((half, width))] * 2 + [block] * n,
        [hidden_all, summed, blocks],
        flops * 2,
    )

    near = swap(theirs, "sub")
    back = [after(x, near) for x in back]
    back = [back[0]] + [rotate(back[s], s) for s in range(1, n)]
    parts = (mine, near, swap(mine, "mp"), swap_both(theirs))
    projected = call(
        project_kernel,
        scalars,
        (*parts, w_qkv),
        [struct((half, 3 * HEAD))] * n,
        [pltpu.VMEM((half, channels), BF16), pltpu.VMEM((n, half, 3 * HEAD), BF16)],
        2 * half * channels * 3 * n * HEAD,
    )
    projected, back = lax.optimization_barrier((projected, back))
    received = [projected[0]] + [rotate(projected[s], s) for s in range(1, n)]
    asked = after(asked, back[1])
    w_near = swap(asked, "mp")
    w_far = swap(w_near, "sub")

    swapped = [swap(x, "sub") for x in received]
    keys = pltpu.VMEM((8 * half, HEAD), BF16)
    *attended, keep, give = call(
        attend_kernel,
        scalars,
        (*received, *swapped, *back),
        [struct((half, HEAD))] * n + [struct((half, width))] * 2,
        [pltpu.VMEM((2, 2, n, b, HEAD), BF16), keys, keys, blocks],
        4 * half * 4 * 8 * half * HEAD,
    )
    got = swap(give, "sub")
    heads = [attended[0]] + [rotate(attended[s], s) for s in range(1, n)]
    others = [swap(heads[0], "mp")]
    heads[2] = after(heads[2], others[0])
    others += [swap(x, "mp") for x in heads[1:]]
    (out,) = call(
        finish_kernel,
        scalars,
        (*heads, *others, keep, got, w_own, w_near, w_far),
        [struct((half, out_width))],
        [pltpu.VMEM((half, 8 * HEAD), BF16), pltpu.VMEM((half, out_width), BF16)],
        2 * half * 8 * HEAD * out_width,
    )
    return out


def passed_along(x, axis, by):
    devices = lax.axis_size(axis)
    pairs = [(i, i + by) for i in range(devices) if 0 <= i + by < devices]
    return lax.ppermute(x, axis, pairs)


def tower_section(stream_shard, gain_row, weight_taps, dilation):
    rows_here = stream_shard.shape[0]
    gathered = lax.all_gather(stream_shard, ("mp", "sub"), axis=1, tiled=True)
    widened = gathered.astype(jnp.float32)
    normed = (
        widened * lax.rsqrt(jnp.mean(widened * widened, axis=1, keepdims=True) + 1e-06) * gain_row
    )
    hidden = jax.nn.gelu(normed).astype(jnp.bfloat16)
    tap_terms = jnp.einsum("rc,jco->jro", hidden, weight_taps, preferred_element_type=jnp.float32)
    span_rows = min(dilation, rows_here)
    hop_count = max(dilation // rows_here, 1)
    lower_part = passed_along(
        tap_terms[0, rows_here - span_rows :].astype(jnp.bfloat16), "seq", hop_count
    ).astype(jnp.float32)
    upper_part = passed_along(
        tap_terms[2, :span_rows].astype(jnp.bfloat16), "seq", -hop_count
    ).astype(jnp.float32)
    before = jnp.concatenate([lower_part, tap_terms[0, : rows_here - span_rows]], axis=0)
    after = jnp.concatenate([tap_terms[2, span_rows:], upper_part], axis=0)
    return (stream_shard.astype(jnp.float32) + before + tap_terms[1] + after).astype(jnp.bfloat16)


def per_device(seq_in, conv_gain, conv_weight, w_q, w_k, w_v, w_o):
    rows_here = seq_in.shape[0]
    dilations = (BINS_DEV // 4, BINS_DEV, 2 * BINS_DEV)
    stream = seq_in
    for section_index in range(LAYERS):
        stream = tower_section(
            stream, conv_gain[section_index], conv_weight[section_index], dilations[section_index]
        )
    query_rows = rows_here // lax.axis_size("sub")
    mp_width = w_o.shape[1] // lax.axis_size("mp")
    widest = lax.all_gather(stream, ("mp", "sub"), axis=1, tiled=True)
    query_inputs = lax.dynamic_slice_in_dim(
        widest, lax.axis_index("sub") * query_rows, query_rows, 0
    )
    residual_part = lax.dynamic_slice_in_dim(
        query_inputs, lax.axis_index("mp") * mp_width, mp_width, 1
    )
    heads_here = w_q.shape[1] // HEAD
    queries = (
        jnp.dot(query_inputs, w_q, preferred_element_type=jnp.float32)
        .astype(jnp.bfloat16)
        .reshape(query_rows, heads_here, HEAD)
    )
    keys = (
        jnp.dot(query_inputs, w_k, preferred_element_type=jnp.float32)
        .astype(jnp.bfloat16)
        .reshape(query_rows, heads_here, HEAD)
    )
    values = (
        jnp.dot(query_inputs, w_v, preferred_element_type=jnp.float32)
        .astype(jnp.bfloat16)
        .reshape(query_rows, heads_here, HEAD)
    )
    score_scale = 1.0 / math.sqrt(HEAD)
    running_top = jnp.full((heads_here, query_rows), -1e30, jnp.float32)
    running_numer = jnp.zeros((query_rows, heads_here, HEAD), jnp.float32)
    key_rows = lax.all_gather(keys, ("seq", "sub"), axis=0, tiled=True)
    value_rows = lax.all_gather(values, ("seq", "sub"), axis=0, tiled=True)
    scores = (
        jnp.einsum("qhe,khe->hqk", queries, key_rows, preferred_element_type=jnp.float32)
        * score_scale
    )
    new_top = jnp.maximum(running_top, jnp.max(scores, axis=-1))
    expw = jnp.exp(scores - new_top[:, :, None])
    factor = jnp.exp(running_top - new_top)
    new_denom = jnp.sum(expw, axis=-1)
    contrib = jnp.einsum(
        "hqk,khe->qhe", expw.astype(jnp.bfloat16), value_rows, preferred_element_type=jnp.float32
    )
    new_numer = running_numer * factor.T[:, :, None] + contrib
    attended = (
        (new_numer / new_denom.T[:, :, None])
        .astype(jnp.bfloat16)
        .reshape(query_rows, heads_here * HEAD)
    )
    column_weight = lax.all_to_all(w_o, "mp", split_axis=1, concat_axis=0, tiled=True)
    every_head = lax.all_gather(attended, "mp", axis=1, tiled=True)
    shares = jnp.dot(every_head, column_weight, preferred_element_type=jnp.float32)
    return (residual_part.astype(jnp.float32) + shares).astype(jnp.bfloat16)


def solution(mesh):
    placed = (
        P(("groups", "seq"), ("mp", "sub")),
        P(),
        P(None, None, None, ("mp", "sub")),
        P(None, "mp"),
        P(None, "mp"),
        P(None, "mp"),
        P("mp", None),
    )
    sizes = dict(mesh.shape)
    dealt = sizes["seq"] == 4 and sizes["mp"] == 2 and sizes["sub"] == 2
    return jax.shard_map(
        per_device_fast if dealt else per_device,
        mesh=mesh,
        in_specs=placed,
        out_specs=P(("groups", "seq", "sub"), "mp"),
        check_vma=False,
    )
```

```python
import functools
import math

import jax
import jax.numpy as jnp
from jax import lax
from jax.experimental import pallas as pl
from jax.experimental.pallas import tpu as pltpu
from jax.sharding import PartitionSpec as P

HEAD = 128
LAYERS = 3
BINS_DEV = 512
F32 = jnp.float32
BF16 = jnp.bfloat16
VMEM_LIMIT = 16 * 1024 * 1024
SPLIT = 4


def swap(x, axis):
    return lax.ppermute(x, axis, [(0, 1), (1, 0)])


def swap_both(x):
    return lax.ppermute(x, ("mp", "sub"), [(i, 3 - i) for i in range(4)])


def rotate(x, by):
    n = lax.axis_size("seq")
    return lax.ppermute(x, "seq", [(i, (i + by) % n) for i in range(n)])


def gather_parts(*pieces, under=None):
    across = [swap(x, "mp") for x in pieces]
    if under is not None:
        across = lax.optimization_barrier((across, under))[0]
    near = [swap(x, "sub") for x in pieces]
    return (*pieces, *near, *across, *[swap(x, "sub") for x in across])


def dot(a, b):
    return jnp.dot(a, b, preferred_element_type=F32)


def at(start, size):
    return pl.ds(pl.multiple_of(start, size), size)


SUB, SEQ, MP = 4, 5, 6


def fill_hidden(scalars, parts, gains, layer, hidden, order=None):
    count = len(parts) // 4
    rows, width = parts[0].shape
    quarter = rows * count // 4
    tile = 16
    columns = [at(scalars[p] * width, width) for p in range(4)]
    gain = [gains[layer : layer + 1, c] for c in columns]
    for r in range(0, rows * count, tile):
        here = slice(r % rows, r % rows + tile)
        wide = [parts[p * count + r // rows][here, :].astype(F32) for p in range(4)]
        squares = wide[0] * wide[0]
        for x in wide[1:]:
            squares = squares + x * x
        mean = jnp.sum(squares, axis=1, keepdims=True) / (4 * width)
        scale = lax.rsqrt(mean + 1e-06)
        if order is None:
            target = pl.ds(r, tile)
        else:
            target = at(order[r // quarter] * quarter + r % quarter, tile)
        for p, x in enumerate(wide):
            hidden[target, columns[p]] = jax.nn.gelu(x * scale * gain[p]).astype(BF16)


def turn(scalars, by):
    return lax.rem(scalars[SEQ] + by, 4)


def bring(copies):
    copies = [pltpu.make_async_copy(*copy) for copy in copies]
    for copy in copies:
        copy.start()
    for copy in copies:
        copy.wait()


def load_taps_kernel(layer, scalars, w, gains, out, gains_out, sems):
    size = out.shape[1] // SPLIT
    copies = [(gains, gains_out, sems.at[3, 0])]
    for tap in range(3):
        for i in range(SPLIT):
            rows = pl.ds(i * size, size)
            copies.append((w.at[layer, tap, rows], out.at[tap, rows], sems.at[tap, i]))
    bring(copies)


def load_projections_kernel(scalars, w_q, w_k, w_v, w_o, out, own, asked, sems):
    size = out.shape[1] // SPLIT
    copies = []
    for m, w in enumerate((w_q, w_k, w_v)):
        for i in range(SPLIT):
            rows = pl.ds(i * size, size)
            copies.append((w.at[rows], out.at[m, rows], sems.at[m, i]))
    half, width = asked.shape
    mp = scalars[MP]
    copies.append((w_o.at[:, at(mp * width, width)], own, sems.at[3, 0]))
    rows = at(scalars[SUB] * half, half)
    copies.append((w_o.at[rows, at((1 - mp) * width, width)], asked, sems.at[3, 1]))
    bring(copies)


def cut_kernel(scalars, x, edge, middle, sems):
    b = edge.shape[0] // 2
    size = 2 * b // SPLIT
    copies = []
    for i in range(SPLIT):
        rows = pl.ds(i * size, size)
        start = i * size if i * size < b else i * size + 2 * b
        copies.append((x.at[pl.ds(start, size)], edge.at[rows], sems.at[0, i]))
        copies.append((x.at[pl.ds(b + i * size, size)], middle.at[rows], sems.at[1, i]))
    bring(copies)


def first_edge_kernel(scalars, p0, p1, p2, p3, gains, w, acc, outer, inner, hidden):
    fill_hidden(scalars, (p0, p1, p2, p3), gains, 0, hidden)
    b = outer.shape[0]
    middle = p0[...].astype(F32) + dot(hidden[...], w[1])
    before = dot(hidden[...], w[0])
    after = dot(hidden[...], w[2])
    odd = lax.rem(scalars[SEQ], 2) == 1
    up, down = before[b:], after[:b]
    outer[...] = jnp.where(odd, down, up).astype(BF16)
    inner[...] = jnp.where(odd, up, down).astype(BF16)
    acc[0] = middle[:b]
    acc[1] = before[:b]
    acc[2] = after[b:]
    acc[3] = middle[b:]


def first_middle_kernel(
    scalars, p0, p1, p2, p3, gains, w, acc, partial, hidden
):
    fill_hidden(scalars, (p0, p1, p2, p3), gains, 0, hidden)
    b = acc.shape[1]
    middle = p0[...].astype(F32) + dot(hidden[...], w[1])
    before = dot(hidden[...], w[0])
    after = dot(hidden[...], w[2])
    partial[0] = acc[0] + after[:b]
    partial[1] = acc[1] + middle[:b] + after[b:]
    partial[2] = acc[2] + middle[b:] + before[:b]
    partial[3] = acc[3] + before[b:]


def deal_kernel(scalars, partial, outer, inner, *refs):
    outs, stream = refs[:4], refs[4]
    odd = lax.rem(scalars[SEQ], 2) == 1
    from_outer, from_inner = outer[...].astype(F32), inner[...].astype(F32)
    lower = jnp.where(odd, from_outer, from_inner)
    upper = jnp.where(odd, from_inner, from_outer)
    stream[0] = (partial[0] + lower).astype(BF16)
    stream[1] = partial[1].astype(BF16)
    stream[2] = partial[2].astype(BF16)
    stream[3] = (partial[3] + upper).astype(BF16)
    for s, out in enumerate(outs):
        out[...] = stream[turn(scalars, s)]


def local_taps(hidden, acc, w, shift):
    rows = hidden.shape[0]
    acc[...] = dot(hidden[...], w[1])
    acc[shift:, :] += dot(hidden[: rows - shift, :], w[0])
    acc[: rows - shift, :] += dot(hidden[shift:, :], w[2])


def second_kernel(scalars, *refs):
    parts = refs[:8]
    gains, w, low, high, hidden, acc, kept = refs[8:]
    half = low.shape[0]
    b = half // 2
    order = [turn(scalars, 4 - s) for s in range(4)]
    fill_hidden(scalars, parts, gains, 1, hidden, order)
    for s in range(4):
        kept[order[s]] = parts[s // 2][(s % 2) * b : (s % 2 + 1) * b, :]
    local_taps(hidden, acc, w, b)
    for k in range(4):
        out = low if k < 2 else high
        made = kept[k].astype(F32) + acc[k * b : (k + 1) * b, :]
        out[(k % 2) * b : (k % 2 + 1) * b, :] = made.astype(BF16)


def third_kernel(scalars, *refs):
    parts = refs[:8]
    gains, w = refs[8:10]
    mine, theirs = refs[10:12]
    outs = refs[12:16]
    hidden, acc, made = refs[16:]
    half = parts[0].shape[0]
    b = half // 2
    fill_hidden(scalars, parts, gains, 2, hidden)
    local_taps(hidden, acc, w, half)
    for k in range(4):
        own = parts[k // 2][(k % 2) * b : (k % 2 + 1) * b, :].astype(F32)
        made[k] = (own + acc[k * b : (k + 1) * b, :]).astype(BF16)
    sub = scalars[SUB]
    for c in range(2):
        rows = slice(c * b, (c + 1) * b)
        mine[rows, :] = made[2 * c + sub]
        theirs[rows, :] = made[2 * c + 1 - sub]
    for s, out in enumerate(outs):
        out[...] = made[turn(scalars, s)]


def project_kernel(scalars, p0, p1, p2, p3, w, o0, o1, o2, o3, rows, made):
    width = p0.shape[1]
    for p, part in enumerate((p0, p1, p2, p3)):
        rows[:, at(scalars[p] * width, width)] = part[...]
    for i in range(3):
        product = dot(rows[...], w[i]).astype(BF16)
        for h in range(4):
            made[h, :, i * HEAD : (i + 1) * HEAD] = product[:, h * HEAD : (h + 1) * HEAD]
    for s, out in enumerate((o0, o1, o2, o3)):
        out[...] = made[turn(scalars, s)]


def attend_kernel(scalars, *refs):
    own, other, arrived, outs = refs[:4], refs[4:8], refs[8:12], refs[12:16]
    keep, give, queries, keys, values, ordered = refs[16:]
    b = own[0].shape[0] // 2
    sub = scalars[SUB]
    for s in range(4):
        ordered[turn(scalars, 4 - s)] = arrived[s][...]
    for a in range(2):
        rows = slice(a * b, (a + 1) * b)
        keep[rows, :] = ordered[2 * sub + a]
        give[rows, :] = ordered[2 * (1 - sub) + a]
    rows = own[0].shape[0]
    for s in range(4):
        for c in range(2):
            queries[c, sub, s] = own[s][c * b : (c + 1) * b, :HEAD]
            queries[c, 1 - sub, s] = other[s][c * b : (c + 1) * b, :HEAD]
        for o, ref in enumerate((own[s], other[s])):
            here = pl.ds((s * 2 + o) * rows, rows)
            keys[here, :] = ref[:, HEAD : 2 * HEAD]
            values[here, :] = ref[:, 2 * HEAD :]
    factor = math.log2(math.e) / math.sqrt(HEAD)
    for s, out in enumerate(outs):
        k = turn(scalars, s)
        asked = jnp.concatenate(
            [
                queries[k // 2, lax.rem(k, 2), lax.rem(scalars[SEQ] - 2 * sub - a + 4, 4)]
                for a in range(2)
            ],
            axis=0,
        )
        scores = lax.dot_general(
            asked, keys[...], (((1,), (1,)), ((), ())), preferred_element_type=F32
        )
        top = jnp.max(scores, axis=1, keepdims=True)
        expw = jnp.exp2((scores - top) * factor)
        denom = jnp.sum(expw, axis=1, keepdims=True)
        numer = dot(expw.astype(BF16), values[...])
        out[...] = (numer / denom).astype(BF16)


def finish_kernel(scalars, *refs):
    own, other = refs[:4], refs[4:8]
    keep, got, w_own, w_near, w_far, out, mixed, residual = refs[8:]
    sub = scalars[SUB]
    width = keep.shape[1]
    half = 4 * HEAD
    for s in range(4):
        head = turn(scalars, 4 - s)
        mixed[:, at(head * HEAD, HEAD)] = own[s][...]
        place = lax.rem(head + 2 * (1 - sub) + 2, 4)
        mixed[:, at(half + place * HEAD, HEAD)] = other[s][...]
    residual[:, at(sub * width, width)] = keep[...]
    residual[:, at((1 - sub) * width, width)] = got[...]
    shares = dot(mixed[:, :half], w_own[...])
    shares = shares + dot(mixed[:, half : half + 2 * HEAD], w_near[...])
    shares = shares + dot(mixed[:, half + 2 * HEAD :], w_far[...])
    out[...] = (residual[...].astype(F32) + shares).astype(BF16)


def whole(x):
    zeros = (0,) * len(x.shape)
    return pl.BlockSpec(x.shape, lambda *_: zeros)


def struct(shape, dtype=BF16):
    return jax.ShapeDtypeStruct(shape, dtype)


def call(kernel, scalars, args, outs, scratch, flops, far=(), limit=VMEM_LIMIT):
    moved = sum(math.prod(a.shape) * a.dtype.itemsize for a in (*args, *outs))
    return pl.pallas_call(
        kernel,
        out_shape=outs,
        grid_spec=pltpu.PrefetchScalarGridSpec(
            num_scalar_prefetch=1,
            grid=(1,),
            in_specs=[
                pl.BlockSpec(memory_space=pltpu.HBM) if i in far else whole(a)
                for i, a in enumerate(args)
            ],
            out_specs=[whole(o) for o in outs],
            scratch_shapes=scratch,
        ),
        compiler_params=pltpu.CompilerParams(
            dimension_semantics=("arbitrary",), vmem_limit_bytes=limit
        ),
        cost_estimate=pl.CostEstimate(flops=flops, transcendentals=0, bytes_accessed=moved),
        name=getattr(kernel, "func", kernel).__name__,
    )(scalars, *args)


def after(x, *earlier):
    return lax.optimization_barrier((x, *earlier))[0]


def per_device_fast(seq_in, conv_gain, conv_weight, w_q, w_k, w_v, w_o):
    seq_in, conv_gain, conv_weight, w_q, w_k, w_v, w_o = (
        pltpu.with_memory_space_constraint(w, pltpu.HBM)
        for w in (seq_in, conv_gain, conv_weight, w_q, w_k, w_v, w_o)
    )
    rows, width = seq_in.shape
    channels = 4 * width
    n = 4
    b = rows // n
    half = rows // 2
    z, mp, sub = (lax.axis_index(a) for a in ("seq", "mp", "sub"))
    place = mp * 2 + sub
    scalars = jnp.stack([place, place ^ 1, place ^ 2, place ^ 3, sub, z, mp]).astype(jnp.int32)
    hidden = pltpu.VMEM((half, channels), BF16)
    hidden_all = pltpu.VMEM((rows, channels), BF16)
    summed = pltpu.VMEM((rows, width), F32)
    blocks = pltpu.VMEM((n, b, width), BF16)
    block = struct((b, width))
    flops = 2 * half * channels * 3 * width
    out_width = w_o.shape[1] // 2
    sems = pltpu.SemaphoreType.DMA((4, SPLIT))

    def load_taps(layer):
        w, gains = call(
            functools.partial(load_taps_kernel, layer),
            scalars,
            (conv_weight, conv_gain),
            [struct(conv_weight.shape[1:]), struct(conv_gain.shape, F32)],
            [sems],
            0,
            far=(0, 1),
        )
        return gains, w

    edge, middle = call(
        cut_kernel,
        scalars,
        (seq_in,),
        [struct((half, width))] * 2,
        [sems],
        0,
        far=(0,),
    )
    taps = load_taps(0)
    edge_across, middle_across = after(swap(edge, "mp"), taps[1]), swap(middle, "mp")
    acc, outer, inner = call(
        first_edge_kernel,
        scalars,
        (edge, swap(edge, "sub"), edge_across, swap(edge_across, "sub"), *taps),
        [struct((n, b, width), F32), block, block],
        [hidden],
        flops,
    )
    outer = lax.ppermute(outer, "seq", [(i, i ^ 1) for i in range(n)])
    inner = lax.ppermute(inner, "seq", [(1, 2), (2, 1)])
    middle_near = swap(middle, "sub")
    (partial,) = call(
        first_middle_kernel,
        scalars,
        (middle, middle_near, middle_across, swap(middle_across, "sub"), *taps, acc),
        [struct((n, b, width), F32)],
        [hidden],
        flops,
    )
    dealt = call(
        deal_kernel,
        scalars,
        (partial, outer, inner),
        [block] * n,
        [blocks],
        0,
    )
    dealt = [dealt[0]] + [rotate(dealt[s], s) for s in range(1, n)]

    taps = load_taps(1)
    early = jnp.concatenate(dealt[:2], axis=0)
    late = jnp.concatenate(dealt[2:], axis=0)
    low, high = call(
        second_kernel,
        scalars,
        (*gather_parts(early, late, under=taps[1]), *taps),
        [struct((half, width))] * 2,
        [hidden_all, summed, blocks],
        flops * 2,
    )
    w_qkv, w_own, asked = call(
        load_projections_kernel,
        scalars,
        (w_q, w_k, w_v, w_o),
        [
            struct((3, *w_q.shape)),
            struct((w_o.shape[0], out_width)),
            struct((w_o.shape[0] // 2, out_width)),
        ],
        [sems],
        0,
        far=(0, 1, 2, 3),
    )
    taps = load_taps(2)
    mine, theirs, *back = call(
        third_kernel,
        scalars,
        (*gather_parts(low, high, under=(taps[1], w_qkv)), *taps),
        [struct((half, width))] * 2 + [block] * n,
        [hidden_all, summed, blocks],
        flops * 2,
    )

    near = swap(theirs, "sub")
    back = [after(x, near) for x in back]
    back = [back[0]] + [rotate(back[s], s) for s in range(1, n)]
    parts = (mine, near, swap(mine, "mp"), swap_both(theirs))
    projected = call(
        project_kernel,
        scalars,
        (*parts, w_qkv),
        [struct((half, 3 * HEAD))] * n,
        [pltpu.VMEM((half, channels), BF16), pltpu.VMEM((n, half, 3 * HEAD), BF16)],
        2 * half * channels * 3 * n * HEAD,
    )
    projected, back = lax.optimization_barrier((projected, back))
    received = [projected[0]] + [rotate(projected[s], s) for s in range(1, n)]
    asked = after(asked, back[1])
    w_near = swap(asked, "mp")
    w_far = swap(w_near, "sub")

    swapped = [swap(x, "sub") for x in received]
    keys = pltpu.VMEM((8 * half, HEAD), BF16)
    *attended, keep, give = call(
        attend_kernel,
        scalars,
        (*received, *swapped, *back),
        [struct((half, HEAD))] * n + [struct((half, width))] * 2,
        [pltpu.VMEM((2, 2, n, b, HEAD), BF16), keys, keys, blocks],
        4 * half * 4 * 8 * half * HEAD,
    )
    got = swap(give, "sub")
    heads = [attended[0]] + [rotate(attended[s], s) for s in range(1, n)]
    others = [swap(x, "mp") for x in heads]
    (out,) = call(
        finish_kernel,
        scalars,
        (*heads, *others, keep, got, w_own, w_near, w_far),
        [struct((half, out_width))],
        [pltpu.VMEM((half, 8 * HEAD), BF16), pltpu.VMEM((half, out_width), BF16)],
        2 * half * 8 * HEAD * out_width,
    )
    return out


def passed_along(x, axis, by):
    devices = lax.axis_size(axis)
    pairs = [(i, i + by) for i in range(devices) if 0 <= i + by < devices]
    return lax.ppermute(x, axis, pairs)


def tower_section(stream_shard, gain_row, weight_taps, dilation):
    rows_here = stream_shard.shape[0]
    gathered = lax.all_gather(stream_shard, ("mp", "sub"), axis=1, tiled=True)
    widened = gathered.astype(jnp.float32)
    normed = (
        widened * lax.rsqrt(jnp.mean(widened * widened, axis=1, keepdims=True) + 1e-06) * gain_row
    )
    hidden = jax.nn.gelu(normed).astype(jnp.bfloat16)
    tap_terms = jnp.einsum("rc,jco->jro", hidden, weight_taps, preferred_element_type=jnp.float32)
    span_rows = min(dilation, rows_here)
    hop_count = max(dilation // rows_here, 1)
    lower_part = passed_along(
        tap_terms[0, rows_here - span_rows :].astype(jnp.bfloat16), "seq", hop_count
    ).astype(jnp.float32)
    upper_part = passed_along(
        tap_terms[2, :span_rows].astype(jnp.bfloat16), "seq", -hop_count
    ).astype(jnp.float32)
    before = jnp.concatenate([lower_part, tap_terms[0, : rows_here - span_rows]], axis=0)
    after = jnp.concatenate([tap_terms[2, span_rows:], upper_part], axis=0)
    return (stream_shard.astype(jnp.float32) + before + tap_terms[1] + after).astype(jnp.bfloat16)


def per_device(seq_in, conv_gain, conv_weight, w_q, w_k, w_v, w_o):
    rows_here = seq_in.shape[0]
    dilations = (BINS_DEV // 4, BINS_DEV, 2 * BINS_DEV)
    stream = seq_in
    for section_index in range(LAYERS):
        stream = tower_section(
            stream, conv_gain[section_index], conv_weight[section_index], dilations[section_index]
        )
    query_rows = rows_here // lax.axis_size("sub")
    mp_width = w_o.shape[1] // lax.axis_size("mp")
    widest = lax.all_gather(stream, ("mp", "sub"), axis=1, tiled=True)
    query_inputs = lax.dynamic_slice_in_dim(
        widest, lax.axis_index("sub") * query_rows, query_rows, 0
    )
    residual_part = lax.dynamic_slice_in_dim(
        query_inputs, lax.axis_index("mp") * mp_width, mp_width, 1
    )
    heads_here = w_q.shape[1] // HEAD
    queries = (
        jnp.dot(query_inputs, w_q, preferred_element_type=jnp.float32)
        .astype(jnp.bfloat16)
        .reshape(query_rows, heads_here, HEAD)
    )
    keys = (
        jnp.dot(query_inputs, w_k, preferred_element_type=jnp.float32)
        .astype(jnp.bfloat16)
        .reshape(query_rows, heads_here, HEAD)
    )
    values = (
        jnp.dot(query_inputs, w_v, preferred_element_type=jnp.float32)
        .astype(jnp.bfloat16)
        .reshape(query_rows, heads_here, HEAD)
    )
    score_scale = 1.0 / math.sqrt(HEAD)
    running_top = jnp.full((heads_here, query_rows), -1e30, jnp.float32)
    running_numer = jnp.zeros((query_rows, heads_here, HEAD), jnp.float32)
    key_rows = lax.all_gather(keys, ("seq", "sub"), axis=0, tiled=True)
    value_rows = lax.all_gather(values, ("seq", "sub"), axis=0, tiled=True)
    scores = (
        jnp.einsum("qhe,khe->hqk", queries, key_rows, preferred_element_type=jnp.float32)
        * score_scale
    )
    new_top = jnp.maximum(running_top, jnp.max(scores, axis=-1))
    expw = jnp.exp(scores - new_top[:, :, None])
    factor = jnp.exp(running_top - new_top)
    new_denom = jnp.sum(expw, axis=-1)
    contrib = jnp.einsum(
        "hqk,khe->qhe", expw.astype(jnp.bfloat16), value_rows, preferred_element_type=jnp.float32
    )
    new_numer = running_numer * factor.T[:, :, None] + contrib
    attended = (
        (new_numer / new_denom.T[:, :, None])
        .astype(jnp.bfloat16)
        .reshape(query_rows, heads_here * HEAD)
    )
    column_weight = lax.all_to_all(w_o, "mp", split_axis=1, concat_axis=0, tiled=True)
    every_head = lax.all_gather(attended, "mp", axis=1, tiled=True)
    shares = jnp.dot(every_head, column_weight, preferred_element_type=jnp.float32)
    return (residual_part.astype(jnp.float32) + shares).astype(jnp.bfloat16)


def solution(mesh):
    placed = (
        P(("groups", "seq"), ("mp", "sub")),
        P(),
        P(None, None, None, ("mp", "sub")),
        P(None, "mp"),
        P(None, "mp"),
        P(None, "mp"),
        P("mp", None),
    )
    sizes = dict(mesh.shape)
    dealt = sizes["seq"] == 4 and sizes["mp"] == 2 and sizes["sub"] == 2
    return jax.shard_map(
        per_device_fast if dealt else per_device,
        mesh=mesh,
        in_specs=placed,
        out_specs=P(("groups", "seq", "sub"), "mp"),
        check_vma=False,
    )
```
